32 devices in a mesh: gx: 4 (over y, x), gy: 2 (over core), gz: 4 (over z).
Axes of the slice: x: 2, y: 2, z: 4, core: 2. Of those that a mesh axis runs over, the one named last changes fastest.
Arguments:
- velocity: float32 [3, 2621440], P(None, ('gx', 'gy', 'gz')), may hold values from -6 to 6
- particle_place: int32 [2621440], P(('gx', 'gy', 'gz')), may hold values from 0 to 8191
- grid_shift: int32 [3], replicated, may hold values from 1 to 3
- rotation_axis: int32 [64, 128, 64], P('gy', 'gx', 'gz'), may hold values from 0 to 1023
Outputs:
- new_velocity: float32 [3, 2621440], P(None, ('gx', 'gy', 'gz'))
- modes: float32 [2, 3, 64, 64, 128], P(None, None, ('gy', 'gz'), 'gx')
- spectrum: float32 [32], replicated
The draws below stay inside these ranges and needn't reach their ends.
Inputs may be any that keep to these rules, and one draw needn't show every extreme that they name: `particle_place`: A device's particle slots come in tiles of 640 slots; tile j holds particles of the device's local cells j * 128 to j * 128 + 127, and a value is (cell within the tile) * 4**3 + (sub-cell code).
All inputs are finite; a program needn't handle non-finite values.
Results may differ from the reference program's by a relative error of at most 0.0005.
Values sent between devices are 32-bit elements; how exact they have to be, the bound alone decides.
A program may use at most 128 MiB of HBM per device.

```python
import math
import jax
import jax.numpy as jnp
from jax import lax

CX = 32
CY = 32
CZ = 16
PPC = 5
TILE = 128
SUB = 4
NAXES = 1024
NX = 128
NY = 64
NZ = 64
NSHELL = 32
PARTS_SIZE = 2621440
N_GY = 2
N_GZ = 4


def plant(array, own_key, smallest, top_value):
    extent = array.shape
    index_at = [jax.random.randint(jax.random.fold_in(own_key, axis), (), 0, extent[axis]) for axis in range(len(extent))]
    array = array.at[tuple(index_at)].set(smallest)
    longest = extent.index(max(extent))
    index_at[longest] = (index_at[longest] + 1) % extent[longest]
    return array.at[tuple(index_at)].set(top_value)


def levels(stream_key, dims, shards, low, largest):
    factor_of = 1.0
    for position, parts in shards:
        steps = jax.random.uniform(jax.random.fold_in(jax.random.fold_in(stream_key, 6), position), (parts,), jnp.float32, low / len(shards), largest / len(shards))
        factor_of = factor_of * jnp.repeat(jnp.exp(steps), dims[position] // parts).reshape((-1,) + (1,) * (len(dims) - 1 - position))
    return factor_of


def scatter_about(rng, dims, scale, most, split=(), held_as=jnp.bfloat16):
    level = levels(rng, dims, split, -0.22, 0.18) if split else 1.0
    array = jax.random.normal(rng, dims, jnp.float32) * scale * level
    return jnp.minimum(jnp.maximum(array, -most), most).astype(held_as)


def setup_inputs(seed: int = 0) -> dict:
    key_of = jax.random.split(jax.random.key(seed), 5)
    return {
        "velocity": scatter_about(key_of[0], (3, PARTS_SIZE), 1.0, 6.0, ((1, 32),), jnp.float32),
        "particle_place": plant(jax.random.randint(key_of[1], (PARTS_SIZE,), 0, TILE * SUB**3), jax.random.fold_in(key_of[1], 1), 0, (TILE * SUB**3) - 1).astype(jnp.int32),
        "grid_shift": jax.random.randint(key_of[2], (3,), 1, SUB).astype(jnp.int32),
        "rotation_axis": plant(jax.random.randint(key_of[3], (NY, NX, NZ), 0, NAXES), jax.random.fold_in(key_of[3], 1), 0, NAXES - 1).astype(jnp.int32),
    }


ROT_COS = math.cos(130.0 * math.pi / 180.0)
ROT_SIN = math.sin(130.0 * math.pi / 180.0)

def axis_vectors(axis_index):
    level = 1.0 - (2.0 * axis_index.astype(jnp.float32) + 1.0) / NAXES
    radius = jnp.sqrt(1.0 - level * level)
    turn = (axis_index * 1597 % 2584).astype(jnp.float32) * (2.0 * math.pi / 2584.0)
    return jnp.stack([radius * jnp.cos(turn), radius * jnp.sin(turn), level])

def collide(particle_speed, cell_mean, normal):
    offset = particle_speed - cell_mean
    across = jnp.cross(normal, offset, axis=0)
    along = lax.optimization_barrier(jnp.sum(normal * offset, axis=0))
    return cell_mean + ROT_COS * offset + ROT_SIN * across + (1.0 - ROT_COS) * along * normal

def signed_wave(length):
    wave = jnp.arange(length, dtype=jnp.int32)
    return jnp.where(wave >= length // 2, wave - length, wave)

def reference(velocity, particle_place, grid_shift, rotation_axis):
    per_device = PPC * CX * CY * CZ
    per_tile = PPC * TILE
    particle_total = velocity.shape[1]
    slot_id = jnp.arange(particle_total, dtype=jnp.int32)
    device = slot_id // per_device
    within = slot_id % per_device
    local_cell = within // per_tile * TILE + particle_place // SUB ** 3
    sub_cell = particle_place % SUB ** 3
    along_x = device // (N_GY * N_GZ)
    along_y = device // N_GZ % N_GY
    along_z = device % N_GZ
    cell_z = along_z * CZ + local_cell % CZ
    cell_x = along_x * CX + local_cell // CZ % CX
    cell_y = along_y * CY + local_cell // (CZ * CX)
    step_x = (sub_cell // (SUB * SUB) + grid_shift[0] >= SUB).astype(jnp.int32)
    step_y = (sub_cell // SUB % SUB + grid_shift[1] >= SUB).astype(jnp.int32)
    step_z = (sub_cell % SUB + grid_shift[2] >= SUB).astype(jnp.int32)
    shifted = ((cell_y + step_y) % NY * NX + (cell_x + step_x) % NX) * NZ + (cell_z + step_z) % NZ
    plain_cell = (cell_y * NX + cell_x) * NZ + cell_z
    cell_total = NX * NY * NZ
    ones = jnp.ones((particle_total,), jnp.float32)
    momentum = jax.ops.segment_sum(velocity.T, shifted, num_segments=cell_total)
    shifted_count = jax.ops.segment_sum(ones, shifted, num_segments=cell_total)
    cell_mean = momentum / jnp.maximum(shifted_count, 1.0)[:, None]
    normal = axis_vectors(rotation_axis.reshape(-1))
    new_speed = collide(velocity, cell_mean[shifted].T, normal[:, shifted])
    plain_sum = jax.ops.segment_sum(new_speed.T, plain_cell, num_segments=cell_total)
    plain_count = jax.ops.segment_sum(ones, plain_cell, num_segments=cell_total)
    cell_velocity = (plain_sum / jnp.maximum(plain_count, 1.0)[:, None]).T.reshape(3, NY, NX, NZ)
    transformed = jnp.fft.fftn(cell_velocity, axes=(1, 2, 3))
    transformed = jnp.transpose(transformed, (0, 3, 1, 2)) / math.sqrt(NX * NY * NZ)
    modes = jnp.stack([jnp.real(transformed), jnp.imag(transformed)]).astype(jnp.float32)
    energy = lax.optimization_barrier(jnp.sum(modes * modes, axis=(0, 1)))
    wave_z = signed_wave(NZ)
    wave_y = signed_wave(NY)
    wave_x = signed_wave(NX)
    square = wave_z[:, None, None] ** 2 + wave_y[None, :, None] ** 2 + wave_x[None, None, :] ** 2
    shell_index = jnp.floor(jnp.sqrt(square.astype(jnp.float32))).astype(jnp.int32)
    shell_index = jnp.minimum(shell_index, NSHELL).reshape(-1)
    shell_sums = jax.ops.segment_sum(energy.reshape(-1), shell_index, num_segments=NSHELL + 1)
    shell_counts = jax.ops.segment_sum(jnp.ones_like(energy.reshape(-1)), shell_index, num_segments=NSHELL + 1)
    spectrum = shell_sums[:NSHELL] / shell_counts[:NSHELL]
    return (new_speed, modes, spectrum)
```

```python
import functools
import math

import jax
import jax.numpy as jnp
from jax import lax
from jax.experimental import pallas as pl
from jax.experimental.pallas import tpu as pltpu
from jax.sharding import PartitionSpec as P

PPC = 5
TILE = 128
SUB = 4
NAXES = 1024

ROT_COS = math.cos(130.0 * math.pi / 180.0)
ROT_SIN = math.sin(130.0 * math.pi / 180.0)
HIGH = lax.Precision.HIGHEST
F32 = jnp.float32
VMEM = pltpu.VMEM


def iota(shape, dim):
    return lax.broadcasted_iota(jnp.int32, shape, dim)


def shift_bits(place, shift_ref):
    code = place & (SUB**3 - 1)
    bit_x = jnp.where((code >> 4) + shift_ref[0] >= SUB, 1, 0)
    bit_y = jnp.where(((code >> 2) & 3) + shift_ref[1] >= SUB, 1, 0)
    bit_z = jnp.where((code & 3) + shift_ref[2] >= SUB, 1, 0)
    return bit_x, bit_y, bit_z


def deposit_kernel(shift_ref, place_ref, v_ref, out_ref):
    place = place_ref[...]
    bit_x, bit_y, bit_z = shift_bits(place, shift_ref)
    octant = bit_x * 4 + bit_y * 2 + bit_z
    member = place >> 6
    sub8 = iota((8, TILE), 0)
    cells = iota((TILE, TILE), 0)
    for tile in range(8):
        lhs = []
        hots = []
        for chunk in range(PPC):
            row = tile * PPC + chunk
            mask = jnp.broadcast_to(octant[row : row + 1], (8, TILE)) == sub8
            parts = []
            for c in range(3):
                value = v_ref[c : c + 1, row * TILE : (row + 1) * TILE]
                high = value.astype(jnp.bfloat16).astype(F32)
                low = value - high
                for part in (high, low):
                    parts.append(jnp.where(mask, jnp.broadcast_to(part, (8, TILE)), 0.0))
            parts.append(jnp.where(mask, 1.0, 0.0))
            parts.append(jnp.zeros((8, TILE), F32))
            lhs.append(jnp.concatenate(parts, axis=0).astype(jnp.bfloat16))
            hot = jnp.broadcast_to(member[row : row + 1], (TILE, TILE)) == cells
            hots.append(jnp.where(hot, 1.0, 0.0).astype(jnp.bfloat16))
        sums = lax.dot_general(
            jnp.concatenate(lhs, axis=1),
            jnp.concatenate(hots, axis=1),
            (((1,), (1,)), ((), ())),
            preferred_element_type=F32,
        )
        for c in range(3):
            out_ref[c, :, tile, :] = sums[16 * c : 16 * c + 8] + sums[16 * c + 8 : 16 * c + 16]
        out_ref[3, :, tile, :] = sums[48:56]


def axis_vectors(index):
    level = 1.0 - (2.0 * index + 1.0) / NAXES
    radius = jnp.sqrt(1.0 - level * level)
    steps = index.astype(jnp.int32) * 1597 % 2584
    turn = steps.astype(F32) * (2.0 * math.pi / 2584.0)
    return radius * jnp.cos(turn), radius * jnp.sin(turn), level


def rotate(offset, n):
    along = (n[0] * offset[0] + n[1] * offset[1] + n[2] * offset[2]) * (1.0 - ROT_COS)
    cross = (
        n[1] * offset[2] - n[2] * offset[1],
        n[2] * offset[0] - n[0] * offset[2],
        n[0] * offset[1] - n[1] * offset[0],
    )
    return [ROT_COS * offset[c] + ROT_SIN * cross[c] + along * n[c] for c in range(3)]


def roll(x, amount, dim=1):
    amount = amount % x.shape[dim]
    return pltpu.roll(x, amount, dim) if amount else x


def take(x, index):
    return jnp.take_along_axis(x, index, axis=1)


def neighbours(name):
    count = lax.axis_size(name)
    me = lax.axis_index(name)
    return lax.rem(me + 1, count), lax.rem(me + count - 1, count)


def halo_kernel(
    s_ref, a_ref, tab_ref, cell_ref,
    y_low, y_up, ya_up, grid_sums, axis_ext, xs, face_sums,
    x_send_up, x_send_down, x_low, x_up, z_send_up, z_send_down, z_low, z_up,
    total, work, tables, send_sem, recv_sem,
):
    rows = 136
    lane = iota((8, TILE), 1)
    sub = iota((8, TILE), 0)
    lane_z = lane & 15

    barrier = pltpu.get_barrier_semaphore()
    for name in ("gx", "gy", "gz"):
        for side in neighbours(name):
            pl.semaphore_signal(
                barrier, inc=1, device_id={name: side}, device_id_type=pl.DeviceIdType.MESH
            )
    pl.semaphore_wait(barrier, 6)

    def remote(src, dst, name, upward, slot):
        up, down = neighbours(name)
        return pltpu.make_async_remote_copy(
            src_ref=src, dst_ref=dst, send_sem=send_sem.at[slot], recv_sem=recv_sem.at[slot],
            device_id={name: up if upward else down}, device_id_type=pl.DeviceIdType.MESH,
        )

    copies = [
        remote(s_ref.at[:, :, 1, :, pl.ds(120, 8), :], y_low, "gy", True, 0),
        remote(s_ref.at[:, :, 0, :, pl.ds(0, 8), :], y_up, "gy", False, 1),
        remote(a_ref.at[pl.ds(0, 8), :], ya_up, "gy", False, 2),
    ]
    for copy in copies:
        copy.start()
    for q in range(4):
        for bx in range(2):
            for bz in range(2):
                grid_sums[q, bx, bz, 8:128, :] = (
                    s_ref[q, bx, 0, bz, 8:128, :] + s_ref[q, bx, 1, bz, 4:124, :]
                )
    axis_ext[0:128, :] = a_ref[...]
    for copy in copies:
        copy.wait()
    for q in range(4):
        for bx in range(2):
            for bz in range(2):
                grid_sums[q, bx, bz, 0:8, :] = s_ref[q, bx, 0, bz, 0:8, :] + jnp.where(
                    sub < 4,
                    roll(y_low[q, bx, bz], 4, 0),
                    roll(s_ref[q, bx, 1, bz, 0:8, :], 4, 0),
                )
                grid_sums[q, bx, bz, 128:136, :] = jnp.where(
                    sub < 4,
                    roll(s_ref[q, bx, 1, bz, 120:128, :], 4, 0) + y_up[q, bx, bz],
                    0.0,
                )
    axis_ext[128:136, :] = jnp.where(sub < 4, ya_up[...], 0.0)

    lane40 = iota((40, TILE), 1)
    zeros40 = jnp.zeros((40, TILE), F32)
    pack_up = zeros40
    pack_down = zeros40
    fill = jnp.zeros((6, TILE), F32)
    for q in range(4):
        for bz in range(2):
            i = q * 2 + bz
            xs[i, 0:8, :] = jnp.zeros((8, TILE), F32)
            xs[i, 136:144, :] = jnp.zeros((8, TILE), F32)
            xs[i, 1:137, :] = roll(grid_sums[q, 1, bz], 16)
            up_rows = jnp.concatenate([xs[i, pl.ds(4, 34, stride=4), :], fill], axis=0)
            down_rows = jnp.concatenate([grid_sums[q, 0, bz, pl.ds(0, 34, stride=4), :], fill], axis=0)
            slot = (lane40 >> 4) == i
            pack_up = jnp.where(slot, roll(up_rows, 16 * i), pack_up)
            pack_down = jnp.where(slot, roll(down_rows, 16 * i), pack_down)
    x_send_up[...] = pack_up
    x_send_down[0] = pack_down
    x_send_down[1] = jnp.concatenate([axis_ext[pl.ds(0, 34, stride=4), :], fill], axis=0)
    copies = [
        remote(x_send_up, x_low, "gx", True, 3),
        remote(x_send_down, x_up, "gx", False, 4),
    ]
    for copy in copies:
        copy.start()
    for copy in copies:
        copy.wait()
    lane_r = iota((rows, TILE), 1)
    from_low = x_low[...]
    for q in range(4):
        for bz in range(2):
            i = q * 2 + bz
            ring = roll(grid_sums[q, 1, bz], 16)
            xs[i, pl.ds(0, 34, stride=4), :] = roll(from_low, -16 * i)[0:34]
            face_sums[q, bz] = grid_sums[q, 0, bz] + jnp.where(lane_r >= 16, ring, xs[i, 0:136, :])
    x32 = pack_up + x_up[0]
    ax32 = x_up[1]

    def squeeze(load, z_pos):
        first = jnp.zeros((8, TILE), F32)
        for k in range(16):
            first = jnp.where(lane_z == k, roll(load(8 * k), k - z_pos), first)
        second = roll(load(128), -z_pos)
        return first, second

    def squeeze_edge(value, from_lane):
        out = jnp.zeros((8, TILE), F32)
        for g in range(5):
            out = jnp.where((lane & 31) == g, roll(value[8 * g : 8 * g + 8], g - from_lane), out)
        return out

    for q in range(4):
        z_send_up[q], z_send_up[4 + q] = squeeze(lambda r: face_sums[q, 1, r : r + 8, :], 15)
        z_send_down[q], z_send_down[4 + q] = squeeze(lambda r: face_sums[q, 0, r : r + 8, :], 0)
    z_send_up[8] = squeeze_edge(x32, 31)
    z_send_down[8] = squeeze_edge(x32, 0)
    z_send_down[9], z_send_down[10] = squeeze(lambda r: axis_ext[r : r + 8, :], 0)
    z_send_down[11] = squeeze_edge(ax32, 0)
    copies = [
        remote(z_send_up, z_low, "gz", True, 5),
        remote(z_send_down, z_up, "gz", False, 6),
    ]
    for copy in copies:
        copy.start()
    for copy in copies:
        copy.wait()

    def spread(buf, q, k):
        return roll(buf[q], -k) if k < 16 else buf[4 + q]

    for q in range(4):
        for k in range(17):
            r = 8 * k
            one = face_sums[q, 1, r : r + 8, :]
            total[0, q, r : r + 8, :] = face_sums[q, 0, r : r + 8, :] + jnp.where(
                lane_z == 0, spread(z_low, q, k), roll(one, 1)
            )
            total[1, q, r : r + 8, :] = roll(one, -15) + spread(z_up, q, k)
    edge = []
    ax_edge = []
    for g in range(5):
        one = x32[8 * g : 8 * g + 8]
        part = lane & 31
        main = one + jnp.where(part == 0, roll(z_low[8], -g), roll(one, -15))
        last = roll(one, -15) + roll(z_up[8], 16 - g)
        edge.append(jnp.where(part == 16, last, main))
        ax_edge.append(jnp.where(lane == 16, roll(z_up[11], 16 - g), ax32[8 * g : 8 * g + 8]))
    edge = jnp.concatenate(edge, axis=0)
    ax_edge = jnp.concatenate(ax_edge, axis=0)

    edge_count = jnp.maximum(roll(edge, -96), 1.0)
    scale = [1.0 / jnp.maximum(total[f, 3], 1.0) for f in range(2)]
    axis_top = jnp.concatenate(
        [roll(z_up[9], -k) for k in range(16)] + [z_up[10]], axis=0
    )
    pick = jnp.clip(lane_r - 32, 0, 7) * 16
    for c in range(4):
        if c < 3:
            inner = total[0, c] * scale[0]
            top = total[1, c] * scale[1]
            side = roll(edge, -32 * c) / edge_count
        else:
            inner, top, side = axis_ext[...], axis_top, ax_edge
        work[0:136, :] = jnp.where(lane_r < 16, inner, roll(top, 16))
        work[136:144, :] = jnp.zeros((8, TILE), F32)
        work[pl.ds(4, 34, stride=4), :] = side[0:34]
        rim = jnp.where(lane_r <= 16, work[1:137, :], take(top, pick))
        if c < 3:
            tables[0, c] = inner
            tables[1, c] = rim
        else:
            in_range = jnp.where((lane_r <= 16) | ((lane_r >= 32) & (lane_r < 40)), rim, 0.0)
            for f, value in enumerate((inner, in_range)):
                for d, vec in enumerate(axis_vectors(value)):
                    tables[f, 3 + d] = vec
    for by in range(2):
        tab_ref[by] = tables[:, :, 4 * by : 4 * by + 128, :]

    xl = lane >> 4

    @pl.loop(0, 16)
    def _(k):
        r = pl.multiple_of(k * 8, 8)
        sums = [jnp.zeros((8, TILE), F32) for _ in range(3)]
        number = jnp.zeros((8, TILE), F32)
        for bx in range(2):
            for bz in range(2):
                x_new, z_new = xl + bx, lane_z + bz
                outside = (x_new == 8) | (z_new == 16)
                rim_at = jnp.where(x_new == 8, z_new, 32 + x_new)
                index = jnp.where(outside, rim_at, (lane + 16 * bx + bz) & 127)
                for by in range(2):
                    got = []
                    for c in range(6):
                        main = tab_ref[by, 0, c, pl.ds(r, 8), :]
                        if bx or bz:
                            rim = tab_ref[by, 1, c, pl.ds(r, 8), :]
                            main = jnp.where(outside, take(rim, index), take(main, index))
                        got.append(main)
                    count = s_ref[3, bx, by, bz, pl.ds(r, 8), :]
                    number = number + count
                    drift = [count * got[c] for c in range(3)]
                    offset = [s_ref[c, bx, by, bz, pl.ds(r, 8), :] - drift[c] for c in range(3)]
                    turned = rotate(offset, got[3:6])
                    sums = [sums[c] + drift[c] + turned[c] for c in range(3)]
        inverse = 1.0 / jnp.maximum(number, 1.0)
        for c in range(3):
            cell_ref[c, pl.ds(r, 8), :] = sums[c] * inverse


def collide_kernel(shift_ref, place_ref, v_ref, tab_ref, out_ref):
    sub = iota((8, TILE), 0)
    for chunk in range(PPC):
        place = place_ref[pl.ds(chunk, 8, stride=PPC), :]
        bit_x, bit_y, bit_z = shift_bits(place, shift_ref)
        cell = place >> 6
        x_new = (cell >> 4) + bit_x
        z_new = (cell & 15) + bit_z
        outside = (x_new == 8) | (z_new == 16)
        rim_at = jnp.where(x_new == 8, z_new, 32 + x_new)
        index = jnp.where(outside, rim_at, (cell + 16 * bit_x + bit_z) & 127)
        upper = bit_y == 1
        got = []
        for c in range(6):
            low = jnp.where(outside, take(tab_ref[0, 1, c], index), take(tab_ref[0, 0, c], index))
            high = jnp.where(outside, take(tab_ref[1, 1, c], index), take(tab_ref[1, 0, c], index))
            got.append(jnp.where(upper, high, low))
        speed = []
        for c in range(3):
            value = jnp.zeros((8, TILE), F32)
            for tile in range(8):
                at = (tile * PPC + chunk) * TILE
                value = jnp.where(
                    sub == tile, jnp.broadcast_to(v_ref[c : c + 1, at : at + TILE], (8, TILE)), value
                )
            speed.append(value)
        turned = rotate([speed[c] - got[c] for c in range(3)], got[3:6])
        for c in range(3):
            value = got[c] + turned[c]
            for tile in range(8):
                at = (tile * PPC + chunk) * TILE
                out_ref[c : c + 1, at : at + TILE] = value[tile : tile + 1]


def deposit(grid_shift, place, velocity, tiles):
    rows = 8 * PPC
    return pl.pallas_call(
        deposit_kernel,
        grid=(tiles // 8,),
        in_specs=[
            pl.BlockSpec(memory_space=pltpu.SMEM),
            pl.BlockSpec((rows, TILE), lambda i: (i, 0)),
            pl.BlockSpec((3, rows * TILE), lambda i: (0, i)),
        ],
        out_specs=pl.BlockSpec((4, 8, 8, TILE), lambda i: (0, 0, i, 0)),
        out_shape=jax.ShapeDtypeStruct((4, 8, tiles, TILE), F32),
        name="deposit",
    )(grid_shift, place, velocity)


def halo(sums, axis, tiles):
    dma = pltpu.SemaphoreType.DMA
    return pl.pallas_call(
        halo_kernel,
        in_specs=[pl.BlockSpec(memory_space=VMEM)] * 2,
        out_specs=[pl.BlockSpec(memory_space=VMEM)] * 2,
        out_shape=[
            jax.ShapeDtypeStruct((2, 2, 6, tiles, TILE), F32),
            jax.ShapeDtypeStruct((3, tiles, TILE), F32),
        ],
        scratch_shapes=[
            VMEM((4, 2, 2, 8, TILE), F32),
            VMEM((4, 2, 2, 8, TILE), F32),
            VMEM((8, TILE), F32),
            VMEM((4, 2, 2, 136, TILE), F32),
            VMEM((136, TILE), F32),
            VMEM((8, 144, TILE), F32),
            VMEM((4, 2, 136, TILE), F32),
            VMEM((40, TILE), F32),
            VMEM((2, 40, TILE), F32),
            VMEM((40, TILE), F32),
            VMEM((2, 40, TILE), F32),
            VMEM((9, 8, TILE), F32),
            VMEM((12, 8, TILE), F32),
            VMEM((9, 8, TILE), F32),
            VMEM((12, 8, TILE), F32),
            VMEM((2, 4, 136, TILE), F32),
            VMEM((144, TILE), F32),
            VMEM((2, 6, 136, TILE), F32),
            dma((7,)),
            dma((7,)),
        ],
        compiler_params=pltpu.CompilerParams(collective_id=0, has_side_effects=True),
        name="halo",
    )(sums, axis)


def collide_particles(grid_shift, place, velocity, tables, tiles):
    rows = 8 * PPC
    return pl.pallas_call(
        collide_kernel,
        grid=(tiles // 8,),
        in_specs=[
            pl.BlockSpec(memory_space=pltpu.SMEM),
            pl.BlockSpec((rows, TILE), lambda i: (i, 0)),
            pl.BlockSpec((3, rows * TILE), lambda i: (0, i)),
            pl.BlockSpec((2, 2, 6, 8, TILE), lambda i: (0, 0, 0, i, 0)),
        ],
        out_specs=pl.BlockSpec((3, rows * TILE), lambda i: (0, i)),
        out_shape=jax.ShapeDtypeStruct(velocity.shape, F32),
        cost_estimate=pl.CostEstimate(flops=60 * velocity.size, bytes_accessed=4000000, transcendentals=0),
        name="collide",
    )(grid_shift, place, velocity, tables)


def phase_tables(positions, length):
    phase_step = positions[..., None] * jnp.arange(length, dtype=jnp.int32) % length
    angle = phase_step.astype(jnp.float32) * (2.0 * math.pi / length)
    return (jnp.cos(angle), jnp.sin(angle))


def signed_wave(first_wave, count_here, length):
    wave = first_wave + jnp.arange(count_here, dtype=jnp.int32)
    return jnp.where(wave >= length // 2, wave - length, wave)


def per_device(velocity, particle_place, grid_shift, rotation_axis):
    size_y, size_x, size_z = rotation_axis.shape
    cell_count = size_y * size_x * size_z
    tile_count = cell_count // TILE
    place = particle_place.reshape(tile_count * PPC, TILE)
    sums = deposit(grid_shift, place, velocity, tile_count)
    axis = rotation_axis.reshape(tile_count, TILE).astype(F32)
    tables, cell_sums = halo(sums.reshape(4, 2, 2, 2, tile_count, TILE), axis, tile_count)
    new_velocity = collide_particles(grid_shift, place, velocity, tables, tile_count)
    cell_velocity = cell_sums.reshape(3, cell_count)
    count_x = lax.axis_size("gx")
    count_y = lax.axis_size("gy")
    count_z = lax.axis_size("gz")
    rows_y = size_y // count_z
    length_x = size_x * count_x
    length_y = size_y * count_y
    length_z = size_z * count_z
    arrived = lax.all_to_all(cell_velocity, "gz", split_axis=1, concat_axis=0, tiled=True)
    arrived = arrived.reshape(count_z, 3, rows_y, size_x, size_z)
    position_z = (
        jnp.arange(count_z, dtype=jnp.int32)[:, None] * size_z
        + jnp.arange(size_z, dtype=jnp.int32)[None, :]
    )
    cos_z, sin_z = phase_tables(position_z, length_z)
    real_z = jnp.einsum("gcyxz,gzk->kcyx", arrived, cos_z, precision=HIGH)
    imag_z = -jnp.einsum("gcyxz,gzk->kcyx", arrived, sin_z, precision=HIGH)
    stacked_z = jnp.stack([real_z, imag_z], axis=1).reshape(length_z, 6, rows_y * size_x)
    pencil = lax.all_to_all(stacked_z, ("gy", "gz"), split_axis=0, concat_axis=1, tiled=True)
    outer_count, outer_step, inner_count, inner_step = (count_y, size_y, count_z, rows_y)
    depth_z = length_z // (count_y * count_z)
    pencil = pencil.reshape(depth_z, outer_count, inner_count, 2, 3, rows_y, size_x)
    position_y = (
        jnp.arange(outer_count, dtype=jnp.int32)[:, None, None] * outer_step
        + jnp.arange(inner_count, dtype=jnp.int32)[None, :, None] * inner_step
        + jnp.arange(rows_y, dtype=jnp.int32)[None, None, :]
    )
    cos_y, sin_y = phase_tables(position_y, length_y)
    part_re = pencil[:, :, :, 0]
    part_im = pencil[:, :, :, 1]
    real_y = jnp.einsum("zabcyx,abyk->kzcx", part_re, cos_y, precision=HIGH) + jnp.einsum(
        "zabcyx,abyk->kzcx", part_im, sin_y, precision=HIGH
    )
    imag_y = jnp.einsum("zabcyx,abyk->kzcx", part_im, cos_y, precision=HIGH) - jnp.einsum(
        "zabcyx,abyk->kzcx", part_re, sin_y, precision=HIGH
    )
    stacked_y = jnp.stack([real_y, imag_y], axis=2).reshape(length_y, depth_z * 6 * size_x)
    columns = lax.all_to_all(stacked_y, "gx", split_axis=0, concat_axis=1, tiled=True)
    depth_y = length_y // count_x
    columns = columns.reshape(depth_y, count_x, depth_z, 2, 3, size_x)
    position_x = (
        jnp.arange(count_x, dtype=jnp.int32)[:, None] * size_x
        + jnp.arange(size_x, dtype=jnp.int32)[None, :]
    )
    cos_x, sin_x = phase_tables(position_x, length_x)
    col_re = columns[:, :, :, 0]
    col_im = columns[:, :, :, 1]
    real_x = jnp.einsum("ygzcx,gxk->czyk", col_re, cos_x, precision=HIGH) + jnp.einsum(
        "ygzcx,gxk->czyk", col_im, sin_x, precision=HIGH
    )
    imag_x = jnp.einsum("ygzcx,gxk->czyk", col_im, cos_x, precision=HIGH) - jnp.einsum(
        "ygzcx,gxk->czyk", col_re, sin_x, precision=HIGH
    )
    norm_scale = 1.0 / math.sqrt(length_x * length_y * length_z)
    modes = jnp.stack([real_x, imag_x], axis=0) * norm_scale
    energy = jnp.sum(modes * modes, axis=(0, 1))
    first_z = (lax.axis_index("gy") * count_z + lax.axis_index("gz")) * depth_z
    first_y = lax.axis_index("gx") * depth_y
    wave_z = signed_wave(first_z, depth_z, length_z)
    wave_y = signed_wave(first_y, depth_y, length_y)
    wave_x = signed_wave(0, length_x, length_x)
    square = wave_z[:, None, None] ** 2 + wave_y[None, :, None] ** 2 + wave_x[None, None, :] ** 2
    shell_index = jnp.floor(jnp.sqrt(square.astype(jnp.float32))).astype(jnp.int32)
    shells = min(min(length_x, length_y), length_z) // 2
    ladder = jnp.arange(shells, dtype=jnp.int32)

    def bin_plane(plane_pair):
        plane_energy, plane_shell = plane_pair
        member_shell = (plane_shell[..., None] == ladder).astype(jnp.float32)
        return (
            jnp.einsum("yx,yxs->s", plane_energy, member_shell, precision=HIGH),
            jnp.sum(member_shell, axis=(0, 1)),
        )

    plane_sums, plane_counts = lax.map(bin_plane, (energy, shell_index))
    shell_totals = lax.psum(
        (jnp.sum(plane_sums, axis=0), jnp.sum(plane_counts, axis=0)), ("gx", "gy", "gz")
    )
    spectrum = shell_totals[0] / shell_totals[1]
    return (new_velocity, modes, spectrum)


def solution(mesh):
    placed = (P(None, ("gx", "gy", "gz")), P(("gx", "gy", "gz")), P(), P("gy", "gx", "gz"))
    return jax.shard_map(
        per_device,
        mesh=mesh,
        in_specs=placed,
        out_specs=(P(None, ("gx", "gy", "gz")), P(None, None, ("gy", "gz"), "gx", None), P()),
        check_vma=False,
    )
```

```python
import functools
import math

import jax
import jax.numpy as jnp
import numpy as np
from jax import lax
from jax.experimental import pallas as pl
from jax.experimental.pallas import tpu as pltpu
from jax.sharding import PartitionSpec as P

PPC = 5
TILE = 128
SUB = 4
NAXES = 1024

ROT_COS = math.cos(130.0 * math.pi / 180.0)
ROT_SIN = math.sin(130.0 * math.pi / 180.0)
HIGH = lax.Precision.HIGH
F32 = jnp.float32
VMEM = pltpu.VMEM


def iota(shape, dim):
    return lax.broadcasted_iota(jnp.int32, shape, dim)


def shift_bits(place, shift_ref):
    code = place & (SUB**3 - 1)
    bit_x = jnp.where((code >> 4) + shift_ref[0] >= SUB, 1, 0)
    bit_y = jnp.where(((code >> 2) & 3) + shift_ref[1] >= SUB, 1, 0)
    bit_z = jnp.where((code & 3) + shift_ref[2] >= SUB, 1, 0)
    return bit_x, bit_y, bit_z


def deposit_kernel(shift_ref, place_ref, v_ref, out_ref):
    place = place_ref[...]
    bit_x, bit_y, bit_z = shift_bits(place, shift_ref)
    octant = bit_x * 4 + bit_y * 2 + bit_z
    member = place >> 6
    sub8 = iota((8, TILE), 0)
    cells = iota((TILE, TILE), 0)
    for tile in range(8):
        lhs = []
        hots = []
        for chunk in range(PPC):
            row = tile * PPC + chunk
            mask = jnp.broadcast_to(octant[row : row + 1], (8, TILE)) == sub8
            parts = []
            for c in range(3):
                value = v_ref[c : c + 1, row * TILE : (row + 1) * TILE]
                high = value.astype(jnp.bfloat16).astype(F32)
                low = value - high
                for part in (high, low):
                    parts.append(jnp.where(mask, jnp.broadcast_to(part, (8, TILE)), 0.0))
            parts.append(jnp.where(mask, 1.0, 0.0))
            parts.append(jnp.zeros((8, TILE), F32))
            lhs.append(jnp.concatenate(parts, axis=0).astype(jnp.bfloat16))
            hot = jnp.broadcast_to(member[row : row + 1], (TILE, TILE)) == cells
            hots.append(jnp.where(hot, 1.0, 0.0).astype(jnp.bfloat16))
        sums = lax.dot_general(
            jnp.concatenate(lhs, axis=1),
            jnp.concatenate(hots, axis=1),
            (((1,), (1,)), ((), ())),
            preferred_element_type=F32,
        )
        for c in range(3):
            out_ref[c, :, tile, :] = sums[16 * c : 16 * c + 8] + sums[16 * c + 8 : 16 * c + 16]
        out_ref[3, :, tile, :] = sums[48:56]


def axis_vectors(index):
    level = 1.0 - (2.0 * index + 1.0) / NAXES
    radius = jnp.sqrt(1.0 - level * level)
    steps = index.astype(jnp.int32) * 1597 % 2584
    turn = steps.astype(F32) * (2.0 * math.pi / 2584.0)
    return radius * jnp.cos(turn), radius * jnp.sin(turn), level


def rotate(offset, n):
    along = (n[0] * offset[0] + n[1] * offset[1] + n[2] * offset[2]) * (1.0 - ROT_COS)
    cross = (
        n[1] * offset[2] - n[2] * offset[1],
        n[2] * offset[0] - n[0] * offset[2],
        n[0] * offset[1] - n[1] * offset[0],
    )
    return [ROT_COS * offset[c] + ROT_SIN * cross[c] + along * n[c] for c in range(3)]


def roll(x, amount, dim=1):
    amount = amount % x.shape[dim]
    return pltpu.roll(x, amount, dim) if amount else x


def take(x, index):
    return jnp.take_along_axis(x, index, axis=1)


def neighbours(name):
    count = lax.axis_size(name)
    me = lax.axis_index(name)
    return lax.rem(me + 1, count), lax.rem(me + count - 1, count)


def halo_kernel(
    s_ref, a_ref, tab_ref, cell_ref,
    y_low, y_up, ya_up, grid_sums, axis_ext, xs, face_sums,
    x_send_up, x_send_down, x_low, x_up, z_send_up, z_send_down, z_low, z_up,
    total, work, tables, send_sem, recv_sem,
):
    rows = 136
    lane = iota((8, TILE), 1)
    sub = iota((8, TILE), 0)
    lane_z = lane & 15

    barrier = pltpu.get_barrier_semaphore()
    for name in ("gx", "gy", "gz"):
        for side in neighbours(name):
            pl.semaphore_signal(
                barrier, inc=1, device_id={name: side}, device_id_type=pl.DeviceIdType.MESH
            )
    pl.semaphore_wait(barrier, 6)

    def remote(src, dst, name, upward, slot):
        up, down = neighbours(name)
        return pltpu.make_async_remote_copy(
            src_ref=src, dst_ref=dst, send_sem=send_sem.at[slot], recv_sem=recv_sem.at[slot],
            device_id={name: up if upward else down}, device_id_type=pl.DeviceIdType.MESH,
        )

    copies = [
        remote(s_ref.at[:, :, 1, :, pl.ds(120, 8), :], y_low, "gy", True, 0),
        remote(s_ref.at[:, :, 0, :, pl.ds(0, 8), :], y_up, "gy", False, 1),
        remote(a_ref.at[pl.ds(0, 8), :], ya_up, "gy", False, 2),
    ]
    for copy in copies:
        copy.start()
    for q in range(4):
        for bx in range(2):
            for bz in range(2):
                grid_sums[q, bx, bz, 8:128, :] = (
                    s_ref[q, bx, 0, bz, 8:128, :] + s_ref[q, bx, 1, bz, 4:124, :]
                )
    axis_ext[0:128, :] = a_ref[...]
    for copy in copies:
        copy.wait()
    for q in range(4):
        for bx in range(2):
            for bz in range(2):
                grid_sums[q, bx, bz, 0:8, :] = s_ref[q, bx, 0, bz, 0:8, :] + jnp.where(
                    sub < 4,
                    roll(y_low[q, bx, bz], 4, 0),
                    roll(s_ref[q, bx, 1, bz, 0:8, :], 4, 0),
                )
                grid_sums[q, bx, bz, 128:136, :] = jnp.where(
                    sub < 4,
                    roll(s_ref[q, bx, 1, bz, 120:128, :], 4, 0) + y_up[q, bx, bz],
                    0.0,
                )
    axis_ext[128:136, :] = jnp.where(sub < 4, ya_up[...], 0.0)

    lane40 = iota((40, TILE), 1)
    zeros40 = jnp.zeros((40, TILE), F32)
    pack_up = zeros40
    pack_down = zeros40
    fill = jnp.zeros((6, TILE), F32)
    for q in range(4):
        for bz in range(2):
            i = q * 2 + bz
            xs[i, 0:8, :] = jnp.zeros((8, TILE), F32)
            xs[i, 136:144, :] = jnp.zeros((8, TILE), F32)
            xs[i, 1:137, :] = roll(grid_sums[q, 1, bz], 16)
            up_rows = jnp.concatenate([xs[i, pl.ds(4, 34, stride=4), :], fill], axis=0)
            down_rows = jnp.concatenate([grid_sums[q, 0, bz, pl.ds(0, 34, stride=4), :], fill], axis=0)
            slot = (lane40 >> 4) == i
            pack_up = jnp.where(slot, roll(up_rows, 16 * i), pack_up)
            pack_down = jnp.where(slot, roll(down_rows, 16 * i), pack_down)
    x_send_up[...] = pack_up
    x_send_down[0] = pack_down
    x_send_down[1] = jnp.concatenate([axis_ext[pl.ds(0, 34, stride=4), :], fill], axis=0)
    copies = [
        remote(x_send_up, x_low, "gx", True, 3),
        remote(x_send_down, x_up, "gx", False, 4),
    ]
    for copy in copies:
        copy.start()
    for copy in copies:
        copy.wait()
    lane_r = iota((rows, TILE), 1)
    from_low = x_low[...]
    for q in range(4):
        for bz in range(2):
            i = q * 2 + bz
            ring = roll(grid_sums[q, 1, bz], 16)
            xs[i, pl.ds(0, 34, stride=4), :] = roll(from_low, -16 * i)[0:34]
            face_sums[q, bz] = grid_sums[q, 0, bz] + jnp.where(lane_r >= 16, ring, xs[i, 0:136, :])
    x32 = pack_up + x_up[0]
    ax32 = x_up[1]

    def squeeze(load, z_pos):
        first = jnp.zeros((8, TILE), F32)
        for k in range(16):
            first = jnp.where(lane_z == k, roll(load(8 * k), k - z_pos), first)
        second = roll(load(128), -z_pos)
        return first, second

    def squeeze_edge(value, from_lane):
        out = jnp.zeros((8, TILE), F32)
        for g in range(5):
            out = jnp.where((lane & 31) == g, roll(value[8 * g : 8 * g + 8], g - from_lane), out)
        return out

    for q in range(4):
        z_send_up[q], z_send_up[4 + q] = squeeze(lambda r: face_sums[q, 1, r : r + 8, :], 15)
        z_send_down[q], z_send_down[4 + q] = squeeze(lambda r: face_sums[q, 0, r : r + 8, :], 0)
    z_send_up[8] = squeeze_edge(x32, 31)
    z_send_down[8] = squeeze_edge(x32, 0)
    z_send_down[9], z_send_down[10] = squeeze(lambda r: axis_ext[r : r + 8, :], 0)
    z_send_down[11] = squeeze_edge(ax32, 0)
    copies = [
        remote(z_send_up, z_low, "gz", True, 5),
        remote(z_send_down, z_up, "gz", False, 6),
    ]
    for copy in copies:
        copy.start()
    for copy in copies:
        copy.wait()

    def spread(buf, q, k):
        return roll(buf[q], -k) if k < 16 else buf[4 + q]

    for q in range(4):
        for k in range(17):
            r = 8 * k
            one = face_sums[q, 1, r : r + 8, :]
            total[0, q, r : r + 8, :] = face_sums[q, 0, r : r + 8, :] + jnp.where(
                lane_z == 0, spread(z_low, q, k), roll(one, 1)
            )
            total[1, q, r : r + 8, :] = roll(one, -15) + spread(z_up, q, k)
    edge = []
    ax_edge = []
    for g in range(5):
        one = x32[8 * g : 8 * g + 8]
        part = lane & 31
        main = one + jnp.where(part == 0, roll(z_low[8], -g), roll(one, -15))
        last = roll(one, -15) + roll(z_up[8], 16 - g)
        edge.append(jnp.where(part == 16, last, main))
        ax_edge.append(jnp.where(lane == 16, roll(z_up[11], 16 - g), ax32[8 * g : 8 * g + 8]))
    edge = jnp.concatenate(edge, axis=0)
    ax_edge = jnp.concatenate(ax_edge, axis=0)

    edge_count = jnp.maximum(roll(edge, -96), 1.0)
    scale = [1.0 / jnp.maximum(total[f, 3], 1.0) for f in range(2)]
    axis_top = jnp.concatenate(
        [roll(z_up[9], -k) for k in range(16)] + [z_up[10]], axis=0
    )
    pick = jnp.clip(lane_r - 32, 0, 7) * 16
    for c in range(4):
        if c < 3:
            inner = total[0, c] * scale[0]
            top = total[1, c] * scale[1]
            side = roll(edge, -32 * c) / edge_count
        else:
            inner, top, side = axis_ext[...], axis_top, ax_edge
        work[0:136, :] = jnp.where(lane_r < 16, inner, roll(top, 16))
        work[136:144, :] = jnp.zeros((8, TILE), F32)
        work[pl.ds(4, 34, stride=4), :] = side[0:34]
        rim = jnp.where(lane_r <= 16, work[1:137, :], take(top, pick))
        if c < 3:
            tables[0, c] = inner
            tables[1, c] = rim
        else:
            in_range = jnp.where((lane_r <= 16) | ((lane_r >= 32) & (lane_r < 40)), rim, 0.0)
            for f, value in enumerate((inner, in_range)):
                for d, vec in enumerate(axis_vectors(value)):
                    tables[f, 3 + d] = vec
    for by in range(2):
        tab_ref[by] = tables[:, :, 4 * by : 4 * by + 128, :]

    xl = lane >> 4

    @pl.loop(0, 16)
    def _(k):
        r = pl.multiple_of(k * 8, 8)
        sums = [jnp.zeros((8, TILE), F32) for _ in range(3)]
        number = jnp.zeros((8, TILE), F32)
        for bx in range(2):
            for bz in range(2):
                x_new, z_new = xl + bx, lane_z + bz
                outside = (x_new == 8) | (z_new == 16)
                rim_at = jnp.where(x_new == 8, z_new, 32 + x_new)
                index = jnp.where(outside, rim_at, (lane + 16 * bx + bz) & 127)
                for by in range(2):
                    got = []
                    for c in range(6):
                        main = tab_ref[by, 0, c, pl.ds(r, 8), :]
                        if bx or bz:
                            rim = tab_ref[by, 1, c, pl.ds(r, 8), :]
                            main = jnp.where(outside, take(rim, index), take(main, index))
                        got.append(main)
                    count = s_ref[3, bx, by, bz, pl.ds(r, 8), :]
                    number = number + count
                    drift = [count * got[c] for c in range(3)]
                    offset = [s_ref[c, bx, by, bz, pl.ds(r, 8), :] - drift[c] for c in range(3)]
                    turned = rotate(offset, got[3:6])
                    sums = [sums[c] + drift[c] + turned[c] for c in range(3)]
        inverse = 1.0 / jnp.maximum(number, 1.0)
        for c in range(3):
            cell_ref[c, pl.ds(r, 8), :] = sums[c] * inverse


def collide_kernel(shift_ref, place_ref, v_ref, tab_ref, out_ref):
    sub = iota((8, TILE), 0)
    for chunk in range(PPC):
        place = place_ref[pl.ds(chunk, 8, stride=PPC), :]
        bit_x, bit_y, bit_z = shift_bits(place, shift_ref)
        cell = place >> 6
        x_new = (cell >> 4) + bit_x
        z_new = (cell & 15) + bit_z
        outside = (x_new == 8) | (z_new == 16)
        rim_at = jnp.where(x_new == 8, z_new, 32 + x_new)
        index = jnp.where(outside, rim_at, (cell + 16 * bit_x + bit_z) & 127)
        upper = bit_y == 1
        got = []
        for c in range(6):
            low = jnp.where(outside, take(tab_ref[0, 1, c], index), take(tab_ref[0, 0, c], index))
            high = jnp.where(outside, take(tab_ref[1, 1, c], index), take(tab_ref[1, 0, c], index))
            got.append(jnp.where(upper, high, low))
        speed = []
        for c in range(3):
            value = jnp.zeros((8, TILE), F32)
            for tile in range(8):
                at = (tile * PPC + chunk) * TILE
                value = jnp.where(
                    sub == tile, jnp.broadcast_to(v_ref[c : c + 1, at : at + TILE], (8, TILE)), value
                )
            speed.append(value)
        turned = rotate([speed[c] - got[c] for c in range(3)], got[3:6])
        for c in range(3):
            value = got[c] + turned[c]
            for tile in range(8):
                at = (tile * PPC + chunk) * TILE
                out_ref[c : c + 1, at : at + TILE] = value[tile : tile + 1]


def deposit(grid_shift, place, velocity, tiles):
    rows = 8 * PPC
    return pl.pallas_call(
        deposit_kernel,
        grid=(tiles // 8,),
        in_specs=[
            pl.BlockSpec(memory_space=pltpu.SMEM),
            pl.BlockSpec((rows, TILE), lambda i: (i, 0)),
            pl.BlockSpec((3, rows * TILE), lambda i: (0, i)),
        ],
        out_specs=pl.BlockSpec((4, 8, 8, TILE), lambda i: (0, 0, i, 0)),
        out_shape=jax.ShapeDtypeStruct((4, 8, tiles, TILE), F32),
        name="deposit",
    )(grid_shift, place, velocity)


def halo(sums, axis, tiles):
    dma = pltpu.SemaphoreType.DMA
    return pl.pallas_call(
        halo_kernel,
        in_specs=[pl.BlockSpec(memory_space=VMEM)] * 2,
        out_specs=[pl.BlockSpec(memory_space=VMEM)] * 2,
        out_shape=[
            jax.ShapeDtypeStruct((2, 2, 6, tiles, TILE), F32),
            jax.ShapeDtypeStruct((3, tiles, TILE), F32),
        ],
        scratch_shapes=[
            VMEM((4, 2, 2, 8, TILE), F32),
            VMEM((4, 2, 2, 8, TILE), F32),
            VMEM((8, TILE), F32),
            VMEM((4, 2, 2, 136, TILE), F32),
            VMEM((136, TILE), F32),
            VMEM((8, 144, TILE), F32),
            VMEM((4, 2, 136, TILE), F32),
            VMEM((40, TILE), F32),
            VMEM((2, 40, TILE), F32),
            VMEM((40, TILE), F32),
            VMEM((2, 40, TILE), F32),
            VMEM((9, 8, TILE), F32),
            VMEM((12, 8, TILE), F32),
            VMEM((9, 8, TILE), F32),
            VMEM((12, 8, TILE), F32),
            VMEM((2, 4, 136, TILE), F32),
            VMEM((144, TILE), F32),
            VMEM((2, 6, 136, TILE), F32),
            dma((7,)),
            dma((7,)),
        ],
        compiler_params=pltpu.CompilerParams(collective_id=0, has_side_effects=True),
        name="halo",
    )(sums, axis)


def collide_particles(grid_shift, place, velocity, tables, tiles):
    rows = 8 * PPC
    return pl.pallas_call(
        collide_kernel,
        grid=(tiles // 8,),
        in_specs=[
            pl.BlockSpec(memory_space=pltpu.SMEM),
            pl.BlockSpec((rows, TILE), lambda i: (i, 0)),
            pl.BlockSpec((3, rows * TILE), lambda i: (0, i)),
            pl.BlockSpec((2, 2, 6, 8, TILE), lambda i: (0, 0, 0, i, 0)),
        ],
        out_specs=pl.BlockSpec((3, rows * TILE), lambda i: (0, i)),
        out_shape=jax.ShapeDtypeStruct(velocity.shape, F32),
        cost_estimate=pl.CostEstimate(flops=60 * velocity.size, bytes_accessed=4000000, transcendentals=0),
        name="collide",
    )(grid_shift, place, velocity, tables)


def shell_kernel(lengths, shells, m_ref, out_ref, bins, mine, others, send_sem, recv_sem):
    names = ("gx", "gy", "gz")
    sizes = [lax.axis_size(name) for name in names]
    at = [lax.axis_index(name) for name in names]
    peers = []
    for dx in range(sizes[0]):
        for dy in range(sizes[1]):
            for dz in range(sizes[2]):
                if dx or dy or dz:
                    peers.append(
                        tuple(lax.rem(at[d] + step, sizes[d]) for d, step in enumerate((dx, dy, dz)))
                    )
    barrier = pltpu.get_barrier_semaphore()
    for peer in peers:
        pl.semaphore_signal(
            barrier, inc=1, device_id=peer, device_id_type=pl.DeviceIdType.MESH
        )
    length_x, length_y, length_z = lengths
    rows = m_ref.shape[2]
    depth_y = length_y // sizes[0]
    depth_z = length_z // (sizes[1] * sizes[2])
    energy = jnp.zeros((rows, length_x), F32)
    for part in range(2):
        for c in range(3):
            value = m_ref[part, c]
            energy = energy + value * value
    row = iota((rows, length_x), 0)
    kz = (at[1] * sizes[2] + at[2]) * depth_z + lax.div(row, depth_y)
    ky = at[0] * depth_y + lax.rem(row, depth_y)
    kx = iota((rows, length_x), 1)
    square = jnp.zeros((rows, length_x), jnp.int32)
    for wave, length in ((kx, length_x), (ky, length_y), (kz, length_z)):
        signed = jnp.where(wave >= length // 2, wave - length, wave)
        square = square + signed * signed
    shell = jnp.floor(jnp.sqrt(square.astype(F32))).astype(jnp.int32)
    shell = jnp.where((shell + 1) * (shell + 1) <= square, shell + 1, shell)
    shell = jnp.where(shell * shell > square, shell - 1, shell)
    for s in range(shells):
        member = shell == s
        bins[0, s : s + 1, :] = jnp.sum(jnp.where(member, energy, 0.0), axis=0, keepdims=True)
        bins[1, s : s + 1, :] = jnp.sum(jnp.where(member, 1.0, 0.0), axis=0, keepdims=True)
    width = bins.shape[2]
    diagonal = iota((shells, width), 0) == iota((shells, width), 1)
    sub = iota((8, width), 0)
    packed = jnp.zeros((8, width), F32)
    for f in range(2):
        column = jnp.sum(bins[f], axis=1, keepdims=True)
        line = jnp.sum(jnp.where(diagonal, column, 0.0), axis=0, keepdims=True)
        packed = jnp.where(sub == f, jnp.broadcast_to(line, (8, width)), packed)
    mine[...] = packed
    pl.semaphore_wait(barrier, len(peers))
    copies = [
        pltpu.make_async_remote_copy(
            src_ref=mine, dst_ref=others.at[slot], send_sem=send_sem.at[slot],
            recv_sem=recv_sem.at[slot], device_id=peer, device_id_type=pl.DeviceIdType.MESH,
        )
        for slot, peer in enumerate(peers)
    ]
    for copy in copies:
        copy.start()
    for copy in copies:
        copy.wait()
    total = packed + jnp.sum(others[...], axis=0)
    out_ref[...] = total / jnp.maximum(roll(total, -1, 0), 1.0)


def shell_spectrum(modes, lengths):
    shells = min(lengths) // 2
    width = lengths[0]
    count = lax.axis_size("gx") * lax.axis_size("gy") * lax.axis_size("gz")
    dma = pltpu.SemaphoreType.DMA
    rows = modes.reshape(2, 3, -1, width)
    out = pl.pallas_call(
        functools.partial(shell_kernel, lengths, shells),
        in_specs=[pl.BlockSpec(memory_space=VMEM)],
        out_specs=pl.BlockSpec(memory_space=VMEM),
        out_shape=jax.ShapeDtypeStruct((8, width), F32),
        scratch_shapes=[
            VMEM((2, shells, width), F32),
            VMEM((8, width), F32),
            VMEM((count - 1, 8, width), F32),
            dma((count - 1,)),
            dma((count - 1,)),
        ],
        compiler_params=pltpu.CompilerParams(collective_id=1, has_side_effects=True),
        name="shells",
    )(rows)
    return out[0, :shells]


def phase_tables(positions, length):
    steps = positions[..., None] * np.arange(length) % length
    angle = steps * (2.0 * math.pi / length)
    return np.cos(angle).astype(np.float32), np.sin(angle).astype(np.float32)


def per_device(velocity, particle_place, grid_shift, rotation_axis):
    size_y, size_x, size_z = rotation_axis.shape
    cell_count = size_y * size_x * size_z
    tile_count = cell_count // TILE
    place = particle_place.reshape(tile_count * PPC, TILE)
    sums = deposit(grid_shift, place, velocity, tile_count)
    axis = rotation_axis.reshape(tile_count, TILE).astype(F32)
    tables, cell_sums = halo(sums.reshape(4, 2, 2, 2, tile_count, TILE), axis, tile_count)
    new_velocity = collide_particles(grid_shift, place, velocity, tables, tile_count)
    cell_velocity = cell_sums.reshape(3, cell_count)
    count_x = lax.axis_size("gx")
    count_y = lax.axis_size("gy")
    count_z = lax.axis_size("gz")
    rows_y = size_y // count_z
    length_x = size_x * count_x
    length_y = size_y * count_y
    length_z = size_z * count_z
    arrived = lax.all_to_all(cell_velocity, "gz", split_axis=1, concat_axis=0, tiled=True)
    arrived = arrived.reshape(count_z, 3, rows_y, size_x, size_z)
    cos_z, sin_z = phase_tables(np.arange(length_z).reshape(count_z, size_z), length_z)
    both_z = np.stack([cos_z, -sin_z], axis=-1)
    stacked_z = jnp.einsum("gcyxz,gzkp->kpcyx", arrived, both_z, precision=HIGH)
    stacked_z = stacked_z.reshape(length_z, 6, rows_y * size_x)
    pencil = lax.all_to_all(stacked_z, ("gy", "gz"), split_axis=0, concat_axis=1, tiled=True)
    depth_z = length_z // (count_y * count_z)
    pencil = pencil.reshape(depth_z, count_y, count_z, 2, 3, rows_y, size_x)
    cos_y, sin_y = phase_tables(np.arange(length_y).reshape(count_y, count_z, rows_y), length_y)
    both_y = np.stack([np.stack([cos_y, -sin_y]), np.stack([sin_y, cos_y])])
    stacked_y = jnp.einsum("zabpcyx,pqabyk->kzqcx", pencil, both_y, precision=HIGH)
    stacked_y = stacked_y.reshape(length_y, depth_z * 6 * size_x)
    columns = lax.all_to_all(stacked_y, "gx", split_axis=0, concat_axis=1, tiled=True)
    depth_y = length_y // count_x
    columns = columns.reshape(depth_y, count_x, depth_z, 2, 3, size_x)
    cos_x, sin_x = phase_tables(np.arange(length_x).reshape(count_x, size_x), length_x)
    norm_scale = 1.0 / math.sqrt(length_x * length_y * length_z)
    both_x = np.stack([np.stack([cos_x, -sin_x]), np.stack([sin_x, cos_x])])
    both_x = (both_x * norm_scale).astype(np.float32)
    modes = jnp.einsum("ygzpcx,pqgxk->qczyk", columns, both_x, precision=HIGH)
    spectrum = shell_spectrum(modes, (length_x, length_y, length_z))
    return (new_velocity, modes, spectrum)


def solution(mesh):
    placed = (P(None, ("gx", "gy", "gz")), P(("gx", "gy", "gz")), P(), P("gy", "gx", "gz"))
    return jax.shard_map(
        per_device,
        mesh=mesh,
        in_specs=placed,
        out_specs=(P(None, ("gx", "gy", "gz")), P(None, None, ("gy", "gz"), "gx", None), P()),
        check_vma=False,
    )
```

```python
import functools
import math

import jax
import jax.numpy as jnp
import numpy as np
from jax import lax
from jax.experimental import pallas as pl
from jax.experimental.pallas import tpu as pltpu
from jax.sharding import PartitionSpec as P

PPC = 5
TILE = 128
SUB = 4
NAXES = 1024

ROT_COS = math.cos(130.0 * math.pi / 180.0)
ROT_SIN = math.sin(130.0 * math.pi / 180.0)
HIGH = lax.Precision.HIGH
F32 = jnp.float32
VMEM = pltpu.VMEM


def iota(shape, dim):
    return lax.broadcasted_iota(jnp.int32, shape, dim)


def shift_bits(place, shift_ref):
    code = place & (SUB**3 - 1)
    bit_x = jnp.where((code >> 4) + shift_ref[0] >= SUB, 1, 0)
    bit_y = jnp.where(((code >> 2) & 3) + shift_ref[1] >= SUB, 1, 0)
    bit_z = jnp.where((code & 3) + shift_ref[2] >= SUB, 1, 0)
    return bit_x, bit_y, bit_z


def deposit_kernel(shift_ref, place_ref, v_ref, out_ref):
    place = place_ref[...]
    bit_x, bit_y, bit_z = shift_bits(place, shift_ref)
    octant = bit_x * 4 + bit_y * 2 + bit_z
    member = place >> 6
    sub8 = iota((8, TILE), 0)
    cells = iota((TILE, TILE), 0)
    for tile in range(8):
        lhs = []
        hots = []
        for chunk in range(PPC):
            row = tile * PPC + chunk
            mask = jnp.broadcast_to(octant[row : row + 1], (8, TILE)) == sub8
            parts = []
            for c in range(3):
                value = v_ref[c : c + 1, row * TILE : (row + 1) * TILE]
                high = value.astype(jnp.bfloat16).astype(F32)
                low = value - high
                for part in (high, low):
                    parts.append(jnp.where(mask, jnp.broadcast_to(part, (8, TILE)), 0.0))
            parts.append(jnp.where(mask, 1.0, 0.0))
            parts.append(jnp.zeros((8, TILE), F32))
            lhs.append(jnp.concatenate(parts, axis=0).astype(jnp.bfloat16))
            hot = jnp.broadcast_to(member[row : row + 1], (TILE, TILE)) == cells
            hots.append(jnp.where(hot, 1.0, 0.0).astype(jnp.bfloat16))
        sums = lax.dot_general(
            jnp.concatenate(lhs, axis=1),
            jnp.concatenate(hots, axis=1),
            (((1,), (1,)), ((), ())),
            preferred_element_type=F32,
        )
        for c in range(3):
            out_ref[c, :, tile, :] = sums[16 * c : 16 * c + 8] + sums[16 * c + 8 : 16 * c + 16]
        out_ref[3, :, tile, :] = sums[48:56]


def axis_vectors(index):
    level = 1.0 - (2.0 * index + 1.0) / NAXES
    radius = jnp.sqrt(1.0 - level * level)
    steps = index.astype(jnp.int32) * 1597 % 2584
    turn = steps.astype(F32) * (2.0 * math.pi / 2584.0)
    return radius * jnp.cos(turn), radius * jnp.sin(turn), level


def rotate(offset, n):
    along = (n[0] * offset[0] + n[1] * offset[1] + n[2] * offset[2]) * (1.0 - ROT_COS)
    cross = (
        n[1] * offset[2] - n[2] * offset[1],
        n[2] * offset[0] - n[0] * offset[2],
        n[0] * offset[1] - n[1] * offset[0],
    )
    return [ROT_COS * offset[c] + ROT_SIN * cross[c] + along * n[c] for c in range(3)]


def roll(x, amount, dim=1):
    amount = amount % x.shape[dim]
    return pltpu.roll(x, amount, dim) if amount else x


def take(x, index):
    return jnp.take_along_axis(x, index, axis=1)


def neighbours(name):
    count = lax.axis_size(name)
    me = lax.axis_index(name)
    return lax.rem(me + 1, count), lax.rem(me + count - 1, count)


def halo_kernel(
    s_ref, a_ref, tab_ref, cell_ref,
    y_low, y_up, ya_up, grid_sums, axis_ext, xs, face_sums,
    x_send_up, x_send_down, x_low, x_up, z_send_up, z_send_down, z_low, z_up,
    total, work, tables, outgoing, incoming, send_sem, recv_sem, cell_send, cell_recv,
):
    rows = 136
    lane = iota((8, TILE), 1)
    sub = iota((8, TILE), 0)
    lane_z = lane & 15

    barrier = pltpu.get_barrier_semaphore()
    count_z = lax.axis_size("gz")
    me_z = lax.axis_index("gz")
    greeted = [("gx", side) for side in neighbours("gx")]
    greeted += [("gy", side) for side in neighbours("gy")]
    greeted += [("gz", lax.rem(me_z + step, count_z)) for step in range(1, count_z)]
    for name, side in greeted:
        pl.semaphore_signal(
            barrier, inc=1, device_id={name: side}, device_id_type=pl.DeviceIdType.MESH
        )
    pl.semaphore_wait(barrier, len(greeted))

    def remote(src, dst, name, upward, slot):
        up, down = neighbours(name)
        return pltpu.make_async_remote_copy(
            src_ref=src, dst_ref=dst, send_sem=send_sem.at[slot], recv_sem=recv_sem.at[slot],
            device_id={name: up if upward else down}, device_id_type=pl.DeviceIdType.MESH,
        )

    copies = [
        remote(s_ref.at[:, :, 1, :, pl.ds(120, 8), :], y_low, "gy", True, 0),
        remote(s_ref.at[:, :, 0, :, pl.ds(0, 8), :], y_up, "gy", False, 1),
        remote(a_ref.at[pl.ds(0, 8), :], ya_up, "gy", False, 2),
    ]
    for copy in copies:
        copy.start()
    for q in range(4):
        for bx in range(2):
            for bz in range(2):
                grid_sums[q, bx, bz, 8:128, :] = (
                    s_ref[q, bx, 0, bz, 8:128, :] + s_ref[q, bx, 1, bz, 4:124, :]
                )
    axis_ext[0:128, :] = a_ref[...]
    for copy in copies:
        copy.wait()
    for q in range(4):
        for bx in range(2):
            for bz in range(2):
                grid_sums[q, bx, bz, 0:8, :] = s_ref[q, bx, 0, bz, 0:8, :] + jnp.where(
                    sub < 4,
                    roll(y_low[q, bx, bz], 4, 0),
                    roll(s_ref[q, bx, 1, bz, 0:8, :], 4, 0),
                )
                grid_sums[q, bx, bz, 128:136, :] = jnp.where(
                    sub < 4,
                    roll(s_ref[q, bx, 1, bz, 120:128, :], 4, 0) + y_up[q, bx, bz],
                    0.0,
                )
    axis_ext[128:136, :] = jnp.where(sub < 4, ya_up[...], 0.0)

    lane40 = iota((40, TILE), 1)
    zeros40 = jnp.zeros((40, TILE), F32)
    pack_up = zeros40
    pack_down = zeros40
    fill = jnp.zeros((6, TILE), F32)
    for q in range(4):
        for bz in range(2):
            i = q * 2 + bz
            xs[i, 0:8, :] = jnp.zeros((8, TILE), F32)
            xs[i, 136:144, :] = jnp.zeros((8, TILE), F32)
            xs[i, 1:137, :] = roll(grid_sums[q, 1, bz], 16)
            up_rows = jnp.concatenate([xs[i, pl.ds(4, 34, stride=4), :], fill], axis=0)
            down_rows = jnp.concatenate([grid_sums[q, 0, bz, pl.ds(0, 34, stride=4), :], fill], axis=0)
            slot = (lane40 >> 4) == i
            pack_up = jnp.where(slot, roll(up_rows, 16 * i), pack_up)
            pack_down = jnp.where(slot, roll(down_rows, 16 * i), pack_down)
    x_send_up[...] = pack_up
    x_send_down[0] = pack_down
    x_send_down[1] = jnp.concatenate([axis_ext[pl.ds(0, 34, stride=4), :], fill], axis=0)
    copies = [
        remote(x_send_up, x_low, "gx", True, 3),
        remote(x_send_down, x_up, "gx", False, 4),
    ]
    for copy in copies:
        copy.start()
    for copy in copies:
        copy.wait()
    lane_r = iota((rows, TILE), 1)
    from_low = x_low[...]
    for q in range(4):
        for bz in range(2):
            i = q * 2 + bz
            ring = roll(grid_sums[q, 1, bz], 16)
            xs[i, pl.ds(0, 34, stride=4), :] = roll(from_low, -16 * i)[0:34]
            face_sums[q, bz] = grid_sums[q, 0, bz] + jnp.where(lane_r >= 16, ring, xs[i, 0:136, :])
    x32 = pack_up + x_up[0]
    ax32 = x_up[1]

    def squeeze(load, z_pos):
        first = jnp.zeros((8, TILE), F32)
        for k in range(16):
            first = jnp.where(lane_z == k, roll(load(8 * k), k - z_pos), first)
        second = roll(load(128), -z_pos)
        return first, second

    def squeeze_edge(value, from_lane):
        out = jnp.zeros((8, TILE), F32)
        for g in range(5):
            out = jnp.where((lane & 31) == g, roll(value[8 * g : 8 * g + 8], g - from_lane), out)
        return out

    for q in range(4):
        z_send_up[q], z_send_up[4 + q] = squeeze(lambda r: face_sums[q, 1, r : r + 8, :], 15)
        z_send_down[q], z_send_down[4 + q] = squeeze(lambda r: face_sums[q, 0, r : r + 8, :], 0)
    z_send_up[8] = squeeze_edge(x32, 31)
    z_send_down[8] = squeeze_edge(x32, 0)
    z_send_down[9], z_send_down[10] = squeeze(lambda r: axis_ext[r : r + 8, :], 0)
    z_send_down[11] = squeeze_edge(ax32, 0)
    copies = [
        remote(z_send_up, z_low, "gz", True, 5),
        remote(z_send_down, z_up, "gz", False, 6),
    ]
    for copy in copies:
        copy.start()
    for copy in copies:
        copy.wait()

    def spread(buf, q, k):
        return roll(buf[q], -k) if k < 16 else buf[4 + q]

    for q in range(4):
        for k in range(17):
            r = 8 * k
            one = face_sums[q, 1, r : r + 8, :]
            total[0, q, r : r + 8, :] = face_sums[q, 0, r : r + 8, :] + jnp.where(
                lane_z == 0, spread(z_low, q, k), roll(one, 1)
            )
            total[1, q, r : r + 8, :] = roll(one, -15) + spread(z_up, q, k)
    edge = []
    ax_edge = []
    for g in range(5):
        one = x32[8 * g : 8 * g + 8]
        part = lane & 31
        main = one + jnp.where(part == 0, roll(z_low[8], -g), roll(one, -15))
        last = roll(one, -15) + roll(z_up[8], 16 - g)
        edge.append(jnp.where(part == 16, last, main))
        ax_edge.append(jnp.where(lane == 16, roll(z_up[11], 16 - g), ax32[8 * g : 8 * g + 8]))
    edge = jnp.concatenate(edge, axis=0)
    ax_edge = jnp.concatenate(ax_edge, axis=0)

    edge_count = jnp.maximum(roll(edge, -96), 1.0)
    scale = [1.0 / jnp.maximum(total[f, 3], 1.0) for f in range(2)]
    axis_top = jnp.concatenate(
        [roll(z_up[9], -k) for k in range(16)] + [z_up[10]], axis=0
    )
    pick = jnp.clip(lane_r - 32, 0, 7) * 16
    for c in range(4):
        if c < 3:
            inner = total[0, c] * scale[0]
            top = total[1, c] * scale[1]
            side = roll(edge, -32 * c) / edge_count
        else:
            inner, top, side = axis_ext[...], axis_top, ax_edge
        work[0:136, :] = jnp.where(lane_r < 16, inner, roll(top, 16))
        work[136:144, :] = jnp.zeros((8, TILE), F32)
        work[pl.ds(4, 34, stride=4), :] = side[0:34]
        rim = jnp.where(lane_r <= 16, work[1:137, :], take(top, pick))
        if c < 3:
            tables[0, c] = inner
            tables[1, c] = rim
        else:
            in_range = jnp.where((lane_r <= 16) | ((lane_r >= 32) & (lane_r < 40)), rim, 0.0)
            for f, value in enumerate((inner, in_range)):
                for d, vec in enumerate(axis_vectors(value)):
                    tables[f, 3 + d] = vec
    for by in range(2):
        tab_ref[by] = tables[:, :, 4 * by : 4 * by + 128, :]

    xl = lane >> 4

    def cell_group(r, slot, row):
        sums = [jnp.zeros((8, TILE), F32) for _ in range(3)]
        number = jnp.zeros((8, TILE), F32)
        for bx in range(2):
            for bz in range(2):
                x_new, z_new = xl + bx, lane_z + bz
                outside = (x_new == 8) | (z_new == 16)
                rim_at = jnp.where(x_new == 8, z_new, 32 + x_new)
                index = jnp.where(outside, rim_at, (lane + 16 * bx + bz) & 127)
                for by in range(2):
                    got = []
                    for c in range(6):
                        main = tab_ref[by, 0, c, pl.ds(r, 8), :]
                        if bx or bz:
                            rim = tab_ref[by, 1, c, pl.ds(r, 8), :]
                            main = jnp.where(outside, take(rim, index), take(main, index))
                        got.append(main)
                    count = s_ref[3, bx, by, bz, pl.ds(r, 8), :]
                    number = number + count
                    drift = [count * got[c] for c in range(3)]
                    offset = [s_ref[c, bx, by, bz, pl.ds(r, 8), :] - drift[c] for c in range(3)]
                    turned = rotate(offset, got[3:6])
                    sums = [sums[c] + drift[c] + turned[c] for c in range(3)]
        inverse = 1.0 / jnp.maximum(number, 1.0)
        for c in range(3):
            outgoing[slot, c, pl.ds(row, 8), :] = sums[c] * inverse

    share = outgoing.shape[2]
    sent = []
    for step in list(range(1, count_z)) + [0]:
        owner = lax.rem(me_z + step, count_z)

        @pl.loop(0, share // 8)
        def _(k):
            row = pl.multiple_of(k * 8, 8)
            cell_group(pl.multiple_of(owner * share + row, 8), step, row)

        if step:
            copy = pltpu.make_async_remote_copy(
                src_ref=outgoing.at[step], dst_ref=incoming.at[step - 1],
                send_sem=cell_send.at[step - 1], recv_sem=cell_recv.at[step - 1],
                device_id={"gz": owner}, device_id_type=pl.DeviceIdType.MESH,
            )
            copy.start()
            sent.append(copy)
    cell_ref[me_z] = outgoing[0]
    for step in range(1, count_z):
        sent[step - 1].wait()
        cell_ref[lax.rem(me_z + count_z - step, count_z)] = incoming[step - 1]


def collide_kernel(shift_ref, place_ref, v_ref, tab_ref, out_ref):
    sub = iota((8, TILE), 0)
    for chunk in range(PPC):
        place = place_ref[pl.ds(chunk, 8, stride=PPC), :]
        bit_x, bit_y, bit_z = shift_bits(place, shift_ref)
        cell = place >> 6
        x_new = (cell >> 4) + bit_x
        z_new = (cell & 15) + bit_z
        outside = (x_new == 8) | (z_new == 16)
        rim_at = jnp.where(x_new == 8, z_new, 32 + x_new)
        index = jnp.where(outside, rim_at, (cell + 16 * bit_x + bit_z) & 127)
        upper = bit_y == 1
        got = []
        for c in range(6):
            low = jnp.where(outside, take(tab_ref[0, 1, c], index), take(tab_ref[0, 0, c], index))
            high = jnp.where(outside, take(tab_ref[1, 1, c], index), take(tab_ref[1, 0, c], index))
            got.append(jnp.where(upper, high, low))
        speed = []
        for c in range(3):
            value = jnp.zeros((8, TILE), F32)
            for tile in range(8):
                at = (tile * PPC + chunk) * TILE
                value = jnp.where(
                    sub == tile, jnp.broadcast_to(v_ref[c : c + 1, at : at + TILE], (8, TILE)), value
                )
            speed.append(value)
        turned = rotate([speed[c] - got[c] for c in range(3)], got[3:6])
        for c in range(3):
            value = got[c] + turned[c]
            for tile in range(8):
                at = (tile * PPC + chunk) * TILE
                out_ref[c : c + 1, at : at + TILE] = value[tile : tile + 1]


def deposit(grid_shift, place, velocity, tiles):
    rows = 8 * PPC
    return pl.pallas_call(
        deposit_kernel,
        grid=(tiles // 8,),
        in_specs=[
            pl.BlockSpec(memory_space=pltpu.SMEM),
            pl.BlockSpec((rows, TILE), lambda i: (i, 0)),
            pl.BlockSpec((3, rows * TILE), lambda i: (0, i)),
        ],
        out_specs=pl.BlockSpec((4, 8, 8, TILE), lambda i: (0, 0, i, 0)),
        out_shape=jax.ShapeDtypeStruct((4, 8, tiles, TILE), F32),
        name="deposit",
    )(grid_shift, place, velocity)


def halo(sums, axis, tiles):
    dma = pltpu.SemaphoreType.DMA
    count_z = lax.axis_size("gz")
    share = tiles // count_z
    return pl.pallas_call(
        halo_kernel,
        in_specs=[pl.BlockSpec(memory_space=VMEM)] * 2,
        out_specs=[pl.BlockSpec(memory_space=VMEM)] * 2,
        out_shape=[
            jax.ShapeDtypeStruct((2, 2, 6, tiles, TILE), F32),
            jax.ShapeDtypeStruct((count_z, 3, share, TILE), F32),
        ],
        scratch_shapes=[
            VMEM((4, 2, 2, 8, TILE), F32),
            VMEM((4, 2, 2, 8, TILE), F32),
            VMEM((8, TILE), F32),
            VMEM((4, 2, 2, 136, TILE), F32),
            VMEM((136, TILE), F32),
            VMEM((8, 144, TILE), F32),
            VMEM((4, 2, 136, TILE), F32),
            VMEM((40, TILE), F32),
            VMEM((2, 40, TILE), F32),
            VMEM((40, TILE), F32),
            VMEM((2, 40, TILE), F32),
            VMEM((9, 8, TILE), F32),
            VMEM((12, 8, TILE), F32),
            VMEM((9, 8, TILE), F32),
            VMEM((12, 8, TILE), F32),
            VMEM((2, 4, 136, TILE), F32),
            VMEM((144, TILE), F32),
            VMEM((2, 6, 136, TILE), F32),
            VMEM((count_z, 3, share, TILE), F32),
            VMEM((count_z - 1, 3, share, TILE), F32),
            dma((7,)),
            dma((7,)),
            dma((count_z - 1,)),
            dma((count_z - 1,)),
        ],
        compiler_params=pltpu.CompilerParams(collective_id=0, has_side_effects=True),
        name="halo",
    )(sums, axis)


def collide_particles(grid_shift, place, velocity, tables, tiles):
    rows = 8 * PPC
    return pl.pallas_call(
        collide_kernel,
        grid=(tiles // 8,),
        in_specs=[
            pl.BlockSpec(memory_space=pltpu.SMEM),
            pl.BlockSpec((rows, TILE), lambda i: (i, 0)),
            pl.BlockSpec((3, rows * TILE), lambda i: (0, i)),
            pl.BlockSpec((2, 2, 6, 8, TILE), lambda i: (0, 0, 0, i, 0)),
        ],
        out_specs=pl.BlockSpec((3, rows * TILE), lambda i: (0, i)),
        out_shape=jax.ShapeDtypeStruct(velocity.shape, F32),
        cost_estimate=pl.CostEstimate(flops=60 * velocity.size, bytes_accessed=4000000, transcendentals=0),
        name="collide",
    )(grid_shift, place, velocity, tables)


def exchange_kernel(x_ref, out_ref, send_sem, recv_sem):
    count_y, count_z = lax.axis_size("gy"), lax.axis_size("gz")
    me_y, me_z = lax.axis_index("gy"), lax.axis_index("gz")
    me = me_y * count_z + me_z
    peers = [
        (lax.rem(me_y + dy, count_y), lax.rem(me_z + dz, count_z))
        for dy in range(count_y)
        for dz in range(count_z)
        if dy or dz
    ]
    barrier = pltpu.get_barrier_semaphore()
    for y, z in peers:
        pl.semaphore_signal(
            barrier, inc=1, device_id={"gy": y, "gz": z}, device_id_type=pl.DeviceIdType.MESH
        )
    pl.semaphore_wait(barrier, len(peers))
    copies = [
        pltpu.make_async_remote_copy(
            src_ref=x_ref.at[y * count_z + z], dst_ref=out_ref.at[me],
            send_sem=send_sem.at[slot], recv_sem=recv_sem.at[slot],
            device_id={"gy": y, "gz": z}, device_id_type=pl.DeviceIdType.MESH,
        )
        for slot, (y, z) in enumerate(peers)
    ]
    for copy in copies:
        copy.start()
    out_ref[me] = x_ref[me]
    for copy in copies:
        copy.wait()


def exchange(blocks):
    peers = blocks.shape[0] - 1
    dma = pltpu.SemaphoreType.DMA
    return pl.pallas_call(
        exchange_kernel,
        in_specs=[pl.BlockSpec(memory_space=VMEM)],
        out_specs=pl.BlockSpec(memory_space=VMEM),
        out_shape=jax.ShapeDtypeStruct(blocks.shape, F32),
        scratch_shapes=[dma((peers,)), dma((peers,))],
        compiler_params=pltpu.CompilerParams(collective_id=2, has_side_effects=True),
        name="exchange",
    )(blocks)


def shell_kernel(lengths, shells, m_ref, n_ref, out_ref, bins, mine, others, send_sem, recv_sem):
    names = ("gx", "gy", "gz")
    sizes = [lax.axis_size(name) for name in names]
    at = [lax.axis_index(name) for name in names]
    peers = []
    for dx in range(sizes[0]):
        for dy in range(sizes[1]):
            for dz in range(sizes[2]):
                if dx or dy or dz:
                    peers.append(
                        tuple(lax.rem(at[d] + step, sizes[d]) for d, step in enumerate((dx, dy, dz)))
                    )
    barrier = pltpu.get_barrier_semaphore()
    for peer in peers:
        pl.semaphore_signal(
            barrier, inc=1, device_id=peer, device_id_type=pl.DeviceIdType.MESH
        )
    length_x, length_y, length_z = lengths
    rows = m_ref.shape[2]
    depth_y = length_y // sizes[0]
    depth_z = length_z // (sizes[1] * sizes[2])
    energy = jnp.zeros((rows, length_x), F32)
    for part in range(2):
        for c in range(3):
            value = m_ref[part, c]
            energy = energy + value * value
    row = iota((rows, length_x), 0)
    kz = (at[1] * sizes[2] + at[2]) * depth_z + lax.div(row, depth_y)
    ky = at[0] * depth_y + lax.rem(row, depth_y)
    kx = iota((rows, length_x), 1)
    square = jnp.zeros((rows, length_x), jnp.int32)
    for wave, length in ((kx, length_x), (ky, length_y), (kz, length_z)):
        signed = jnp.where(wave >= length // 2, wave - length, wave)
        square = square + signed * signed
    shell = jnp.floor(jnp.sqrt(square.astype(F32))).astype(jnp.int32)
    shell = jnp.where((shell + 1) * (shell + 1) <= square, shell + 1, shell)
    shell = jnp.where(shell * shell > square, shell - 1, shell)
    for s in range(shells):
        member = shell == s
        bins[s : s + 1, :] = jnp.sum(jnp.where(member, energy, 0.0), axis=0, keepdims=True)
    width = bins.shape[1]
    diagonal = iota((shells, width), 0) == iota((shells, width), 1)
    column = jnp.sum(bins[...], axis=1, keepdims=True)
    line = jnp.sum(jnp.where(diagonal, column, 0.0), axis=0, keepdims=True)
    packed = jnp.broadcast_to(line, (8, width))
    mine[...] = packed
    pl.semaphore_wait(barrier, len(peers))
    copies = [
        pltpu.make_async_remote_copy(
            src_ref=mine, dst_ref=others.at[slot], send_sem=send_sem.at[slot],
            recv_sem=recv_sem.at[slot], device_id=peer, device_id_type=pl.DeviceIdType.MESH,
        )
        for slot, peer in enumerate(peers)
    ]
    for copy in copies:
        copy.start()
    for copy in copies:
        copy.wait()
    total = packed + jnp.sum(others[...], axis=0)
    out_ref[...] = total / n_ref[...]


def shell_spectrum(modes, lengths):
    shells = min(lengths) // 2
    width = lengths[0]
    count = lax.axis_size("gx") * lax.axis_size("gy") * lax.axis_size("gz")
    dma = pltpu.SemaphoreType.DMA
    rows = modes.reshape(2, 3, -1, width)
    waves = [np.minimum(np.arange(n), n - np.arange(n)) ** 2 for n in lengths]
    square = waves[2][:, None, None] + waves[1][None, :, None] + waves[0][None, None, :]
    shell = np.floor(np.sqrt(square.astype(np.float64))).astype(np.int64).ravel()
    number = np.ones((8, width), np.float32)
    number[:, :shells] = np.bincount(shell, minlength=shells)[:shells]
    out = pl.pallas_call(
        functools.partial(shell_kernel, lengths, shells),
        in_specs=[pl.BlockSpec(memory_space=VMEM)] * 2,
        out_specs=pl.BlockSpec(memory_space=VMEM),
        out_shape=jax.ShapeDtypeStruct((8, width), F32),
        scratch_shapes=[
            VMEM((shells, width), F32),
            VMEM((8, width), F32),
            VMEM((count - 1, 8, width), F32),
            dma((count - 1,)),
            dma((count - 1,)),
        ],
        compiler_params=pltpu.CompilerParams(collective_id=1, has_side_effects=True),
        name="shells",
    )(rows, jnp.asarray(number))
    return out[0, :shells]


def phase_tables(positions, length):
    steps = positions[..., None] * np.arange(length) % length
    angle = steps * (2.0 * math.pi / length)
    return np.cos(angle).astype(np.float32), np.sin(angle).astype(np.float32)


def per_device(velocity, particle_place, grid_shift, rotation_axis):
    size_y, size_x, size_z = rotation_axis.shape
    cell_count = size_y * size_x * size_z
    tile_count = cell_count // TILE
    place = particle_place.reshape(tile_count * PPC, TILE)
    sums = deposit(grid_shift, place, velocity, tile_count)
    axis = rotation_axis.reshape(tile_count, TILE).astype(F32)
    tables, cell_sums = halo(sums.reshape(4, 2, 2, 2, tile_count, TILE), axis, tile_count)
    new_velocity = collide_particles(grid_shift, place, velocity, tables, tile_count)
    count_x = lax.axis_size("gx")
    count_y = lax.axis_size("gy")
    count_z = lax.axis_size("gz")
    rows_y = size_y // count_z
    length_x = size_x * count_x
    length_y = size_y * count_y
    length_z = size_z * count_z
    arrived = cell_sums.reshape(count_z, 3, rows_y, size_x, size_z)
    cos_z, sin_z = phase_tables(np.arange(length_z).reshape(count_z, size_z), length_z)
    both_z = np.stack([cos_z, -sin_z], axis=-1)
    stacked_z = jnp.einsum("gcyxz,gzkp->kpcyx", arrived, both_z, precision=HIGH)
    depth_z = length_z // (count_y * count_z)
    pencil = exchange(stacked_z.reshape(count_y * count_z, -1, TILE))
    pencil = pencil.reshape(count_y, count_z, depth_z, 2, 3, rows_y, size_x)
    cos_y, sin_y = phase_tables(np.arange(length_y).reshape(count_y, count_z, rows_y), length_y)
    both_y = np.stack([np.stack([cos_y, -sin_y]), np.stack([sin_y, cos_y])])
    stacked_y = jnp.einsum("abzpcyx,pqabyk->kzqcx", pencil, both_y, precision=HIGH)
    stacked_y = stacked_y.reshape(length_y, depth_z * 6 * size_x)
    columns = lax.all_to_all(stacked_y, "gx", split_axis=0, concat_axis=1, tiled=True)
    depth_y = length_y // count_x
    columns = columns.reshape(depth_y, count_x, depth_z, 2, 3, size_x)
    cos_x, sin_x = phase_tables(np.arange(length_x).reshape(count_x, size_x), length_x)
    norm_scale = 1.0 / math.sqrt(length_x * length_y * length_z)
    both_x = np.stack([np.stack([cos_x, -sin_x]), np.stack([sin_x, cos_x])])
    both_x = (both_x * norm_scale).astype(np.float32)
    modes = jnp.einsum("ygzpcx,pqgxk->qczyk", columns, both_x, precision=HIGH)
    spectrum = shell_spectrum(modes, (length_x, length_y, length_z))
    return (new_velocity, modes, spectrum)


def solution(mesh):
    placed = (P(None, ("gx", "gy", "gz")), P(("gx", "gy", "gz")), P(), P("gy", "gx", "gz"))
    return jax.shard_map(
        per_device,
        mesh=mesh,
        in_specs=placed,
        out_specs=(P(None, ("gx", "gy", "gz")), P(None, None, ("gy", "gz"), "gx", None), P()),
        check_vma=False,
    )
```

```python
import functools
import math

import jax
import jax.numpy as jnp
import numpy as np
from jax import lax
from jax.experimental import pallas as pl
from jax.experimental.pallas import tpu as pltpu
from jax.sharding import PartitionSpec as P

PPC = 5
TILE = 128
SUB = 4
NAXES = 1024

ROT_COS = math.cos(130.0 * math.pi / 180.0)
ROT_SIN = math.sin(130.0 * math.pi / 180.0)
HIGH = lax.Precision.HIGH
F32 = jnp.float32
VMEM = pltpu.VMEM


def iota(shape, dim):
    return lax.broadcasted_iota(jnp.int32, shape, dim)


def shift_bits(place, shift_ref):
    code = place & (SUB**3 - 1)
    bit_x = jnp.where((code >> 4) + shift_ref[0] >= SUB, 1, 0)
    bit_y = jnp.where(((code >> 2) & 3) + shift_ref[1] >= SUB, 1, 0)
    bit_z = jnp.where((code & 3) + shift_ref[2] >= SUB, 1, 0)
    return bit_x, bit_y, bit_z


def deposit_kernel(shift_ref, place_ref, v_ref, out_ref):
    place = place_ref[...]
    bit_x, bit_y, bit_z = shift_bits(place, shift_ref)
    octant = bit_x * 4 + bit_y * 2 + bit_z
    member = place >> 6
    sub8 = iota((8, TILE), 0)
    cells = iota((TILE, TILE), 0)
    for tile in range(8):
        lhs = []
        hots = []
        for chunk in range(PPC):
            row = tile * PPC + chunk
            mask = jnp.broadcast_to(octant[row : row + 1], (8, TILE)) == sub8
            parts = []
            for c in range(3):
                value = v_ref[c : c + 1, row * TILE : (row + 1) * TILE]
                high = value.astype(jnp.bfloat16).astype(F32)
                low = value - high
                for part in (high, low):
                    parts.append(jnp.where(mask, jnp.broadcast_to(part, (8, TILE)), 0.0))
            parts.append(jnp.where(mask, 1.0, 0.0))
            parts.append(jnp.zeros((8, TILE), F32))
            lhs.append(jnp.concatenate(parts, axis=0).astype(jnp.bfloat16))
            hot = jnp.broadcast_to(member[row : row + 1], (TILE, TILE)) == cells
            hots.append(jnp.where(hot, 1.0, 0.0).astype(jnp.bfloat16))
        sums = lax.dot_general(
            jnp.concatenate(lhs, axis=1),
            jnp.concatenate(hots, axis=1),
            (((1,), (1,)), ((), ())),
            preferred_element_type=F32,
        )
        for c in range(3):
            out_ref[c, :, tile, :] = sums[16 * c : 16 * c + 8] + sums[16 * c + 8 : 16 * c + 16]
        out_ref[3, :, tile, :] = sums[48:56]


def axis_vectors(index):
    level = 1.0 - (2.0 * index + 1.0) / NAXES
    radius = jnp.sqrt(1.0 - level * level)
    steps = index.astype(jnp.int32) * 1597 % 2584
    turn = steps.astype(F32) * (2.0 * math.pi / 2584.0)
    return radius * jnp.cos(turn), radius * jnp.sin(turn), level


def rotate(offset, n):
    along = (n[0] * offset[0] + n[1] * offset[1] + n[2] * offset[2]) * (1.0 - ROT_COS)
    cross = (
        n[1] * offset[2] - n[2] * offset[1],
        n[2] * offset[0] - n[0] * offset[2],
        n[0] * offset[1] - n[1] * offset[0],
    )
    return [ROT_COS * offset[c] + ROT_SIN * cross[c] + along * n[c] for c in range(3)]


def roll(x, amount, dim=1):
    amount = amount % x.shape[dim]
    return pltpu.roll(x, amount, dim) if amount else x


def take(x, index):
    return jnp.take_along_axis(x, index, axis=1)


def neighbours(name):
    count = lax.axis_size(name)
    me = lax.axis_index(name)
    return lax.rem(me + 1, count), lax.rem(me + count - 1, count)


def halo_kernel(
    s_ref, a_ref, tab_ref, cell_ref,
    y_low, y_up, ya_up, grid_sums, axis_ext, xs, face_sums,
    x_send_up, x_send_down, x_low, x_up, z_send_up, z_send_down, z_low, z_up,
    total, work, tables, outgoing, incoming, send_sem, recv_sem, cell_send, cell_recv,
):
    rows = 136
    lane = iota((8, TILE), 1)
    sub = iota((8, TILE), 0)
    lane_z = lane & 15

    barrier = pltpu.get_barrier_semaphore()
    count_z = lax.axis_size("gz")
    me_z = lax.axis_index("gz")
    greeted = [("gx", side) for side in neighbours("gx")]
    greeted += [("gy", side) for side in neighbours("gy")]
    greeted += [("gz", lax.rem(me_z + step, count_z)) for step in range(1, count_z)]
    for name, side in greeted:
        pl.semaphore_signal(
            barrier, inc=1, device_id={name: side}, device_id_type=pl.DeviceIdType.MESH
        )
    pl.semaphore_wait(barrier, len(greeted))

    def remote(src, dst, name, upward, slot):
        up, down = neighbours(name)
        return pltpu.make_async_remote_copy(
            src_ref=src, dst_ref=dst, send_sem=send_sem.at[slot], recv_sem=recv_sem.at[slot],
            device_id={name: up if upward else down}, device_id_type=pl.DeviceIdType.MESH,
        )

    copies = [
        remote(s_ref.at[:, :, 1, :, pl.ds(120, 8), :], y_low, "gy", True, 0),
        remote(s_ref.at[:, :, 0, :, pl.ds(0, 8), :], y_up, "gy", False, 1),
        remote(a_ref.at[pl.ds(0, 8), :], ya_up, "gy", False, 2),
    ]
    for copy in copies:
        copy.start()
    for q in range(4):
        for bx in range(2):
            for bz in range(2):
                grid_sums[q, bx, bz, 8:128, :] = (
                    s_ref[q, bx, 0, bz, 8:128, :] + s_ref[q, bx, 1, bz, 4:124, :]
                )
    axis_ext[0:128, :] = a_ref[...]
    for copy in copies:
        copy.wait()
    for q in range(4):
        for bx in range(2):
            for bz in range(2):
                grid_sums[q, bx, bz, 0:8, :] = s_ref[q, bx, 0, bz, 0:8, :] + jnp.where(
                    sub < 4,
                    roll(y_low[q, bx, bz], 4, 0),
                    roll(s_ref[q, bx, 1, bz, 0:8, :], 4, 0),
                )
                grid_sums[q, bx, bz, 128:136, :] = jnp.where(
                    sub < 4,
                    roll(s_ref[q, bx, 1, bz, 120:128, :], 4, 0) + y_up[q, bx, bz],
                    0.0,
                )
    axis_ext[128:136, :] = jnp.where(sub < 4, ya_up[...], 0.0)

    lane40 = iota((40, TILE), 1)
    zeros40 = jnp.zeros((40, TILE), F32)
    pack_up = zeros40
    pack_down = zeros40
    fill = jnp.zeros((6, TILE), F32)
    for q in range(4):
        for bz in range(2):
            i = q * 2 + bz
            xs[i, 0:8, :] = jnp.zeros((8, TILE), F32)
            xs[i, 136:144, :] = jnp.zeros((8, TILE), F32)
            xs[i, 1:137, :] = roll(grid_sums[q, 1, bz], 16)
            up_rows = jnp.concatenate([xs[i, pl.ds(4, 34, stride=4), :], fill], axis=0)
            down_rows = jnp.concatenate([grid_sums[q, 0, bz, pl.ds(0, 34, stride=4), :], fill], axis=0)
            slot = (lane40 >> 4) == i
            pack_up = jnp.where(slot, roll(up_rows, 16 * i), pack_up)
            pack_down = jnp.where(slot, roll(down_rows, 16 * i), pack_down)
    x_send_up[...] = pack_up
    x_send_down[0] = pack_down
    x_send_down[1] = jnp.concatenate([axis_ext[pl.ds(0, 34, stride=4), :], fill], axis=0)
    copies = [
        remote(x_send_up, x_low, "gx", True, 3),
        remote(x_send_down, x_up, "gx", False, 4),
    ]
    for copy in copies:
        copy.start()
    for copy in copies:
        copy.wait()
    lane_r = iota((rows, TILE), 1)
    from_low = x_low[...]
    for q in range(4):
        for bz in range(2):
            i = q * 2 + bz
            ring = roll(grid_sums[q, 1, bz], 16)
            xs[i, pl.ds(0, 34, stride=4), :] = roll(from_low, -16 * i)[0:34]
            face_sums[q, bz] = grid_sums[q, 0, bz] + jnp.where(lane_r >= 16, ring, xs[i, 0:136, :])
    x32 = pack_up + x_up[0]
    ax32 = x_up[1]

    def squeeze(load, z_pos):
        first = jnp.zeros((8, TILE), F32)
        for k in range(16):
            first = jnp.where(lane_z == k, roll(load(8 * k), k - z_pos), first)
        second = roll(load(128), -z_pos)
        return first, second

    def squeeze_edge(value, from_lane):
        out = jnp.zeros((8, TILE), F32)
        for g in range(5):
            out = jnp.where((lane & 31) == g, roll(value[8 * g : 8 * g + 8], g - from_lane), out)
        return out

    for q in range(4):
        z_send_up[q], z_send_up[4 + q] = squeeze(lambda r: face_sums[q, 1, r : r + 8, :], 15)
        z_send_down[q], z_send_down[4 + q] = squeeze(lambda r: face_sums[q, 0, r : r + 8, :], 0)
    z_send_up[8] = squeeze_edge(x32, 31)
    z_send_down[8] = squeeze_edge(x32, 0)
    z_send_down[9], z_send_down[10] = squeeze(lambda r: axis_ext[r : r + 8, :], 0)
    z_send_down[11] = squeeze_edge(ax32, 0)
    copies = [
        remote(z_send_up, z_low, "gz", True, 5),
        remote(z_send_down, z_up, "gz", False, 6),
    ]
    for copy in copies:
        copy.start()
    for copy in copies:
        copy.wait()

    def spread(buf, q, k):
        return roll(buf[q], -k) if k < 16 else buf[4 + q]

    for q in range(4):
        for k in range(17):
            r = 8 * k
            one = face_sums[q, 1, r : r + 8, :]
            total[0, q, r : r + 8, :] = face_sums[q, 0, r : r + 8, :] + jnp.where(
                lane_z == 0, spread(z_low, q, k), roll(one, 1)
            )
            total[1, q, r : r + 8, :] = roll(one, -15) + spread(z_up, q, k)
    edge = []
    ax_edge = []
    for g in range(5):
        one = x32[8 * g : 8 * g + 8]
        part = lane & 31
        main = one + jnp.where(part == 0, roll(z_low[8], -g), roll(one, -15))
        last = roll(one, -15) + roll(z_up[8], 16 - g)
        edge.append(jnp.where(part == 16, last, main))
        ax_edge.append(jnp.where(lane == 16, roll(z_up[11], 16 - g), ax32[8 * g : 8 * g + 8]))
    edge = jnp.concatenate(edge, axis=0)
    ax_edge = jnp.concatenate(ax_edge, axis=0)

    edge_count = jnp.maximum(roll(edge, -96), 1.0)
    scale = [1.0 / jnp.maximum(total[f, 3], 1.0) for f in range(2)]
    axis_top = jnp.concatenate(
        [roll(z_up[9], -k) for k in range(16)] + [z_up[10]], axis=0
    )
    pick = jnp.clip(lane_r - 32, 0, 7) * 16
    for c in range(4):
        if c < 3:
            inner = total[0, c] * scale[0]
            top = total[1, c] * scale[1]
            side = roll(edge, -32 * c) / edge_count
        else:
            inner, top, side = axis_ext[...], axis_top, ax_edge
        work[0:136, :] = jnp.where(lane_r < 16, inner, roll(top, 16))
        work[136:144, :] = jnp.zeros((8, TILE), F32)
        work[pl.ds(4, 34, stride=4), :] = side[0:34]
        rim = jnp.where(lane_r <= 16, work[1:137, :], take(top, pick))
        if c < 3:
            tables[0, c] = inner
            tables[1, c] = rim
        else:
            in_range = jnp.where((lane_r <= 16) | ((lane_r >= 32) & (lane_r < 40)), rim, 0.0)
            for f, value in enumerate((inner, in_range)):
                for d, vec in enumerate(axis_vectors(value)):
                    tables[f, 3 + d] = vec
    for by in range(2):
        tab_ref[by] = tables[:, :, 4 * by : 4 * by + 128, :]

    xl = lane >> 4

    def cell_group(r, slot, row):
        sums = [jnp.zeros((8, TILE), F32) for _ in range(3)]
        number = jnp.zeros((8, TILE), F32)
        for bx in range(2):
            for bz in range(2):
                x_new, z_new = xl + bx, lane_z + bz
                outside = (x_new == 8) | (z_new == 16)
                rim_at = jnp.where(x_new == 8, z_new, 32 + x_new)
                index = jnp.where(outside, rim_at, (lane + 16 * bx + bz) & 127)
                for by in range(2):
                    got = []
                    for c in range(6):
                        main = tab_ref[by, 0, c, pl.ds(r, 8), :]
                        if bx or bz:
                            rim = tab_ref[by, 1, c, pl.ds(r, 8), :]
                            main = jnp.where(outside, take(rim, index), take(main, index))
                        got.append(main)
                    count = s_ref[3, bx, by, bz, pl.ds(r, 8), :]
                    number = number + count
                    drift = [count * got[c] for c in range(3)]
                    offset = [s_ref[c, bx, by, bz, pl.ds(r, 8), :] - drift[c] for c in range(3)]
                    turned = rotate(offset, got[3:6])
                    sums = [sums[c] + drift[c] + turned[c] for c in range(3)]
        inverse = 1.0 / jnp.maximum(number, 1.0)
        for c in range(3):
            outgoing[slot, c, pl.ds(row, 8), :] = sums[c] * inverse

    share = outgoing.shape[2]
    sent = []
    for step in list(range(1, count_z)) + [0]:
        owner = lax.rem(me_z + step, count_z)

        @pl.loop(0, share // 8)
        def _(k):
            row = pl.multiple_of(k * 8, 8)
            cell_group(pl.multiple_of(owner * share + row, 8), step, row)

        if step:
            copy = pltpu.make_async_remote_copy(
                src_ref=outgoing.at[step], dst_ref=incoming.at[step - 1],
                send_sem=cell_send.at[step - 1], recv_sem=cell_recv.at[step - 1],
                device_id={"gz": owner}, device_id_type=pl.DeviceIdType.MESH,
            )
            copy.start()
            sent.append(copy)
    cell_ref[me_z] = outgoing[0]
    for step in range(1, count_z):
        sent[step - 1].wait()
        cell_ref[lax.rem(me_z + count_z - step, count_z)] = incoming[step - 1]


def collide_group(group, shift_ref, place_ref, v_ref, tab_ref, out_ref):
    sub = iota((8, TILE), 0)
    tiles = pl.ds(pl.multiple_of(group * 8, 8), 8)
    base = group * (8 * PPC * TILE)
    for chunk in range(PPC):
        place = place_ref[pl.ds(group * (8 * PPC) + chunk, 8, stride=PPC), :]
        bit_x, bit_y, bit_z = shift_bits(place, shift_ref)
        cell = place >> 6
        x_new = (cell >> 4) + bit_x
        z_new = (cell & 15) + bit_z
        outside = (x_new == 8) | (z_new == 16)
        rim_at = jnp.where(x_new == 8, z_new, 32 + x_new)
        index = jnp.where(outside, rim_at, (cell + 16 * bit_x + bit_z) & 127)
        upper = bit_y == 1
        got = []
        for c in range(6):
            low = jnp.where(outside, take(tab_ref[0, 1, c, tiles, :], index), take(tab_ref[0, 0, c, tiles, :], index))
            high = jnp.where(outside, take(tab_ref[1, 1, c, tiles, :], index), take(tab_ref[1, 0, c, tiles, :], index))
            got.append(jnp.where(upper, high, low))
        speed = []
        for c in range(3):
            value = jnp.zeros((8, TILE), F32)
            for tile in range(8):
                at = pl.ds(pl.multiple_of(base + (tile * PPC + chunk) * TILE, TILE), TILE)
                value = jnp.where(
                    sub == tile, jnp.broadcast_to(v_ref[c : c + 1, at], (8, TILE)), value
                )
            speed.append(value)
        turned = rotate([speed[c] - got[c] for c in range(3)], got[3:6])
        for c in range(3):
            value = got[c] + turned[c]
            for tile in range(8):
                at = pl.ds(pl.multiple_of(base + (tile * PPC + chunk) * TILE, TILE), TILE)
                out_ref[c : c + 1, at] = value[tile : tile + 1]


def deposit(grid_shift, place, velocity, tiles):
    rows = 8 * PPC
    return pl.pallas_call(
        deposit_kernel,
        grid=(tiles // 8,),
        in_specs=[
            pl.BlockSpec(memory_space=pltpu.SMEM),
            pl.BlockSpec((rows, TILE), lambda i: (i, 0)),
            pl.BlockSpec((3, rows * TILE), lambda i: (0, i)),
        ],
        out_specs=pl.BlockSpec((4, 8, 8, TILE), lambda i: (0, 0, i, 0)),
        out_shape=jax.ShapeDtypeStruct((4, 8, tiles, TILE), F32),
        name="deposit",
    )(grid_shift, place, velocity)


def halo(sums, axis, tiles):
    dma = pltpu.SemaphoreType.DMA
    count_z = lax.axis_size("gz")
    share = tiles // count_z
    return pl.pallas_call(
        halo_kernel,
        in_specs=[pl.BlockSpec(memory_space=VMEM)] * 2,
        out_specs=[pl.BlockSpec(memory_space=VMEM)] * 2,
        out_shape=[
            jax.ShapeDtypeStruct((2, 2, 6, tiles, TILE), F32),
            jax.ShapeDtypeStruct((count_z, 3, share, TILE), F32),
        ],
        scratch_shapes=[
            VMEM((4, 2, 2, 8, TILE), F32),
            VMEM((4, 2, 2, 8, TILE), F32),
            VMEM((8, TILE), F32),
            VMEM((4, 2, 2, 136, TILE), F32),
            VMEM((136, TILE), F32),
            VMEM((8, 144, TILE), F32),
            VMEM((4, 2, 136, TILE), F32),
            VMEM((40, TILE), F32),
            VMEM((2, 40, TILE), F32),
            VMEM((40, TILE), F32),
            VMEM((2, 40, TILE), F32),
            VMEM((9, 8, TILE), F32),
            VMEM((12, 8, TILE), F32),
            VMEM((9, 8, TILE), F32),
            VMEM((12, 8, TILE), F32),
            VMEM((2, 4, 136, TILE), F32),
            VMEM((144, TILE), F32),
            VMEM((2, 6, 136, TILE), F32),
            VMEM((count_z, 3, share, TILE), F32),
            VMEM((count_z - 1, 3, share, TILE), F32),
            dma((7,)),
            dma((7,)),
            dma((count_z - 1,)),
            dma((count_z - 1,)),
        ],
        compiler_params=pltpu.CompilerParams(collective_id=0, has_side_effects=True),
        name="halo",
    )(sums, axis)


def exchange_kernel(x_ref, out_ref, send_sem, recv_sem):
    count_y, count_z = lax.axis_size("gy"), lax.axis_size("gz")
    me_y, me_z = lax.axis_index("gy"), lax.axis_index("gz")
    me = me_y * count_z + me_z
    peers = [
        (lax.rem(me_y + dy, count_y), lax.rem(me_z + dz, count_z))
        for dy in range(count_y)
        for dz in range(count_z)
        if dy or dz
    ]
    barrier = pltpu.get_barrier_semaphore()
    for y, z in peers:
        pl.semaphore_signal(
            barrier, inc=1, device_id={"gy": y, "gz": z}, device_id_type=pl.DeviceIdType.MESH
        )
    pl.semaphore_wait(barrier, len(peers))
    copies = [
        pltpu.make_async_remote_copy(
            src_ref=x_ref.at[y * count_z + z], dst_ref=out_ref.at[me],
            send_sem=send_sem.at[slot], recv_sem=recv_sem.at[slot],
            device_id={"gy": y, "gz": z}, device_id_type=pl.DeviceIdType.MESH,
        )
        for slot, (y, z) in enumerate(peers)
    ]
    for copy in copies:
        copy.start()
    out_ref[me] = x_ref[me]
    for copy in copies:
        copy.wait()


def exchange(blocks):
    peers = blocks.shape[0] - 1
    dma = pltpu.SemaphoreType.DMA
    return pl.pallas_call(
        exchange_kernel,
        in_specs=[pl.BlockSpec(memory_space=VMEM)],
        out_specs=pl.BlockSpec(memory_space=VMEM),
        out_shape=jax.ShapeDtypeStruct(blocks.shape, F32),
        scratch_shapes=[dma((peers,)), dma((peers,))],
        compiler_params=pltpu.CompilerParams(collective_id=2, has_side_effects=True),
        name="exchange",
    )(blocks)


def final_kernel(
    lengths, shells, shift_ref, place_ref, v_ref, tab_ref, block_ref, phase_ref, n_ref,
    new_ref, m_ref, out_ref,
    arrived, bins, mine, others, block_send, block_recv, send_sem, recv_sem,
):
    groups = place_ref.shape[0] // (8 * PPC)
    cuts = [0, groups // 4, groups * 3 // 4, groups]

    def collide_some(part):
        @pl.loop(cuts[part], cuts[part + 1])
        def _(group):
            collide_group(group, shift_ref, place_ref, v_ref, tab_ref, new_ref)

    names = ("gx", "gy", "gz")
    sizes = [lax.axis_size(name) for name in names]
    at = [lax.axis_index(name) for name in names]
    peers = []
    for dx in range(sizes[0]):
        for dy in range(sizes[1]):
            for dz in range(sizes[2]):
                if dx or dy or dz:
                    peers.append(
                        tuple(lax.rem(at[d] + step, sizes[d]) for d, step in enumerate((dx, dy, dz)))
                    )
    barrier = pltpu.get_barrier_semaphore()
    for peer in peers:
        pl.semaphore_signal(
            barrier, inc=1, device_id=peer, device_id_type=pl.DeviceIdType.MESH
        )
    collide_some(0)
    pl.semaphore_wait(barrier, len(peers))
    blocks = []
    for step in range(1, sizes[0]):
        target = lax.rem(at[0] + step, sizes[0])
        copy = pltpu.make_async_remote_copy(
            src_ref=block_ref.at[target], dst_ref=arrived.at[step - 1],
            send_sem=block_send.at[step - 1], recv_sem=block_recv.at[step - 1],
            device_id={"gx": target}, device_id_type=pl.DeviceIdType.MESH,
        )
        copy.start()
        blocks.append(copy)
    collide_some(1)
    for copy in blocks:
        copy.wait()
    length_x, length_y, length_z = lengths
    half = block_ref.shape[1]
    modes = jnp.zeros((half, 4 * length_x), F32)
    for step in range(sizes[0]):
        source = lax.rem(at[0] + sizes[0] - step, sizes[0])
        value = arrived[step - 1] if step else block_ref[source]
        high = value.astype(jnp.bfloat16)
        low = (value - high.astype(F32)).astype(jnp.bfloat16)
        for left, right in ((high, 0), (low, 0), (high, 1)):
            modes = modes + jnp.dot(left, phase_ref[right, source], preferred_element_type=F32)
    for h in range(2):
        for part in range(2):
            at_lane = (2 * h + part) * length_x
            m_ref[part, h * half : (h + 1) * half, :] = modes[:, at_lane : at_lane + length_x]
    rows = 2 * half // 3
    depth_y = length_y // sizes[0]
    depth_z = length_z // (sizes[1] * sizes[2])
    energy = jnp.zeros((rows, length_x), F32)
    for part in range(2):
        for c in range(3):
            value = m_ref[part, c * rows : (c + 1) * rows, :]
            energy = energy + value * value
    row = iota((rows, length_x), 0)
    kz = (at[1] * sizes[2] + at[2]) * depth_z + lax.div(row, depth_y)
    ky = at[0] * depth_y + lax.rem(row, depth_y)
    kx = iota((rows, length_x), 1)
    square = jnp.zeros((rows, length_x), jnp.int32)
    for wave, length in ((kx, length_x), (ky, length_y), (kz, length_z)):
        signed = jnp.where(wave >= length // 2, wave - length, wave)
        square = square + signed * signed
    shell = jnp.floor(jnp.sqrt(square.astype(F32))).astype(jnp.int32)
    shell = jnp.where((shell + 1) * (shell + 1) <= square, shell + 1, shell)
    shell = jnp.where(shell * shell > square, shell - 1, shell)
    for s in range(shells):
        member = shell == s
        bins[s : s + 1, :] = jnp.sum(jnp.where(member, energy, 0.0), axis=0, keepdims=True)
    width = bins.shape[1]
    diagonal = iota((shells, width), 0) == iota((shells, width), 1)
    column = jnp.sum(bins[...], axis=1, keepdims=True)
    line = jnp.sum(jnp.where(diagonal, column, 0.0), axis=0, keepdims=True)
    packed = jnp.broadcast_to(line, (8, width))
    mine[...] = packed
    copies = [
        pltpu.make_async_remote_copy(
            src_ref=mine, dst_ref=others.at[slot], send_sem=send_sem.at[slot],
            recv_sem=recv_sem.at[slot], device_id=peer, device_id_type=pl.DeviceIdType.MESH,
        )
        for slot, peer in enumerate(peers)
    ]
    for copy in copies:
        copy.start()
    collide_some(2)
    for copy in copies:
        copy.wait()
    total = packed + jnp.sum(others[...], axis=0)
    out_ref[...] = total / n_ref[...]


def finish(grid_shift, place, velocity, tables, blocks, phases, lengths):
    shells = min(lengths) // 2
    width = lengths[0]
    count_x = lax.axis_size("gx")
    count = count_x * lax.axis_size("gy") * lax.axis_size("gz")
    dma = pltpu.SemaphoreType.DMA
    half = blocks.shape[1]
    waves = [np.minimum(np.arange(n), n - np.arange(n)) ** 2 for n in lengths]
    square = waves[2][:, None, None] + waves[1][None, :, None] + waves[0][None, None, :]
    shell = np.floor(np.sqrt(square.astype(np.float64))).astype(np.int64).ravel()
    number = np.ones((8, width), np.float32)
    number[:, :shells] = np.bincount(shell, minlength=shells)[:shells]
    whole = pl.BlockSpec(memory_space=VMEM)
    new_velocity, modes, out = pl.pallas_call(
        functools.partial(final_kernel, lengths, shells),
        in_specs=[pl.BlockSpec(memory_space=pltpu.SMEM)] + [whole] * 6,
        out_specs=[whole] * 3,
        out_shape=[
            jax.ShapeDtypeStruct(velocity.shape, F32),
            jax.ShapeDtypeStruct((2, 2 * half, width), F32),
            jax.ShapeDtypeStruct((8, width), F32),
        ],
        scratch_shapes=[
            VMEM((count_x - 1, half, blocks.shape[2]), F32),
            VMEM((shells, width), F32),
            VMEM((8, width), F32),
            VMEM((count - 1, 8, width), F32),
            dma((count_x - 1,)),
            dma((count_x - 1,)),
            dma((count - 1,)),
            dma((count - 1,)),
        ],
        compiler_params=pltpu.CompilerParams(collective_id=1, has_side_effects=True),
        name="finish",
    )(grid_shift, place, velocity, tables, blocks, phases, jnp.asarray(number))
    return new_velocity, modes, out[0, :shells]


def phase_tables(positions, length):
    steps = positions[..., None] * np.arange(length) % length
    angle = steps * (2.0 * math.pi / length)
    return np.cos(angle).astype(np.float32), np.sin(angle).astype(np.float32)


def per_device(velocity, particle_place, grid_shift, rotation_axis):
    size_y, size_x, size_z = rotation_axis.shape
    cell_count = size_y * size_x * size_z
    tile_count = cell_count // TILE
    place = particle_place.reshape(tile_count * PPC, TILE)
    sums = deposit(grid_shift, place, velocity, tile_count)
    axis = rotation_axis.reshape(tile_count, TILE).astype(F32)
    tables, cell_sums = halo(sums.reshape(4, 2, 2, 2, tile_count, TILE), axis, tile_count)
    count_x = lax.axis_size("gx")
    count_y = lax.axis_size("gy")
    count_z = lax.axis_size("gz")
    rows_y = size_y // count_z
    length_x = size_x * count_x
    length_y = size_y * count_y
    length_z = size_z * count_z
    arrived = cell_sums.reshape(count_z, 3, rows_y, size_x, size_z)
    cos_z, sin_z = phase_tables(np.arange(length_z).reshape(count_z, size_z), length_z)
    both_z = np.stack([cos_z, -sin_z], axis=-1)
    stacked_z = jnp.einsum("gcyxz,gzkp->kpcyx", arrived, both_z, precision=HIGH)
    depth_z = length_z // (count_y * count_z)
    pencil = exchange(stacked_z.reshape(count_y * count_z, -1, TILE))
    pencil = pencil.reshape(count_y, count_z, depth_z, 2, 3, rows_y, size_x)
    cos_y, sin_y = phase_tables(np.arange(length_y).reshape(count_y, count_z, rows_y), length_y)
    both_y = np.stack([np.stack([cos_y, -sin_y]), np.stack([sin_y, cos_y])])
    depth_y = length_y // count_x
    half = 3 * depth_z * depth_y // 2
    stacked_y = jnp.einsum("abzpcyx,pqabyk->czkqx", pencil, both_y, precision=HIGH)
    blocks = stacked_y.reshape(3, depth_z, count_x, depth_y, 2 * size_x)
    blocks = blocks.transpose(2, 0, 1, 3, 4).reshape(count_x, 2, half, 2 * size_x)
    blocks = blocks.transpose(0, 2, 1, 3).reshape(count_x, half, 4 * size_x)
    cos_x, sin_x = phase_tables(np.arange(length_x).reshape(count_x, size_x), length_x)
    norm_scale = 1.0 / math.sqrt(length_x * length_y * length_z)
    both_x = np.stack([np.stack([cos_x, -sin_x]), np.stack([sin_x, cos_x])]) * norm_scale
    both_x = both_x.transpose(2, 0, 3, 1, 4).reshape(count_x, 2 * size_x, 2 * length_x)
    phases = np.zeros((count_x, 4 * size_x, 4 * length_x), np.float32)
    phases[:, : 2 * size_x, : 2 * length_x] = both_x
    phases[:, 2 * size_x :, 2 * length_x :] = both_x
    high = phases.astype(jnp.bfloat16)
    low = (phases - high.astype(np.float32)).astype(jnp.bfloat16)
    new_velocity, modes, spectrum = finish(
        grid_shift, place, velocity, tables, blocks, jnp.asarray(np.stack([high, low])),
        (length_x, length_y, length_z),
    )
    return (new_velocity, modes.reshape(2, 3, depth_z, depth_y, length_x), spectrum)


def solution(mesh):
    placed = (P(None, ("gx", "gy", "gz")), P(("gx", "gy", "gz")), P(), P("gy", "gx", "gz"))
    return jax.shard_map(
        per_device,
        mesh=mesh,
        in_specs=placed,
        out_specs=(P(None, ("gx", "gy", "gz")), P(None, None, ("gy", "gz"), "gx", None), P()),
        check_vma=False,
    )
```

```python
import functools
import math

import jax
import jax.numpy as jnp
import numpy as np
from jax import lax
from jax.experimental import pallas as pl
from jax.experimental.pallas import tpu as pltpu
from jax.sharding import PartitionSpec as P

PPC = 5
TILE = 128
SUB = 4
NAXES = 1024

ROT_COS = math.cos(130.0 * math.pi / 180.0)
ROT_SIN = math.sin(130.0 * math.pi / 180.0)
HIGH = lax.Precision.HIGH
F32 = jnp.float32
VMEM = pltpu.VMEM


def iota(shape, dim):
    return lax.broadcasted_iota(jnp.int32, shape, dim)


def shift_bits(place, shift_ref):
    code = place & (SUB**3 - 1)
    bit_x = jnp.where((code >> 4) + shift_ref[0] >= SUB, 1, 0)
    bit_y = jnp.where(((code >> 2) & 3) + shift_ref[1] >= SUB, 1, 0)
    bit_z = jnp.where((code & 3) + shift_ref[2] >= SUB, 1, 0)
    return bit_x, bit_y, bit_z


def deposit_kernel(shift_ref, place_ref, v_ref, out_ref):
    place = place_ref[...]
    bit_x, bit_y, bit_z = shift_bits(place, shift_ref)
    octant = bit_x * 4 + bit_y * 2 + bit_z
    member = (place >> 6).astype(F32).astype(jnp.bfloat16)
    sub8 = iota((8, TILE), 0)
    cells = iota((TILE, TILE), 0).astype(F32).astype(jnp.bfloat16)
    one = jnp.ones((), jnp.bfloat16)
    zero = jnp.zeros((), jnp.bfloat16)
    for tile in range(8):
        lhs = []
        hots = []
        for chunk in range(PPC):
            row = tile * PPC + chunk
            mask = jnp.broadcast_to(octant[row : row + 1], (8, TILE)) == sub8
            parts = []
            for c in range(3):
                value = v_ref[c : c + 1, row * TILE : (row + 1) * TILE]
                high = value.astype(jnp.bfloat16).astype(F32)
                low = value - high
                for part in (high, low):
                    parts.append(jnp.where(mask, jnp.broadcast_to(part, (8, TILE)), 0.0))
            parts.append(jnp.where(mask, 1.0, 0.0))
            parts.append(jnp.zeros((8, TILE), F32))
            lhs.append(jnp.concatenate(parts, axis=0).astype(jnp.bfloat16))
            hot = jnp.broadcast_to(member[row : row + 1], (TILE, TILE)) == cells
            hots.append(jnp.where(hot, one, zero))
        sums = lax.dot_general(
            jnp.concatenate(lhs, axis=1),
            jnp.concatenate(hots, axis=1),
            (((1,), (1,)), ((), ())),
            preferred_element_type=F32,
        )
        for c in range(3):
            out_ref[c, :, tile, :] = sums[16 * c : 16 * c + 8] + sums[16 * c + 8 : 16 * c + 16]
        out_ref[3, :, tile, :] = sums[48:56]


def axis_vectors(index):
    level = 1.0 - (2.0 * index + 1.0) / NAXES
    radius = jnp.sqrt(1.0 - level * level)
    steps = index.astype(jnp.int32) * 1597 % 2584
    turn = steps.astype(F32) * (2.0 * math.pi / 2584.0)
    return radius * jnp.cos(turn), radius * jnp.sin(turn), level


def rotate(offset, n):
    along = (n[0] * offset[0] + n[1] * offset[1] + n[2] * offset[2]) * (1.0 - ROT_COS)
    cross = (
        n[1] * offset[2] - n[2] * offset[1],
        n[2] * offset[0] - n[0] * offset[2],
        n[0] * offset[1] - n[1] * offset[0],
    )
    return [ROT_COS * offset[c] + ROT_SIN * cross[c] + along * n[c] for c in range(3)]


def roll(x, amount, dim=1):
    amount = amount % x.shape[dim]
    return pltpu.roll(x, amount, dim) if amount else x


def take(x, index):
    return jnp.take_along_axis(x, index, axis=1)


def neighbours(name):
    count = lax.axis_size(name)
    me = lax.axis_index(name)
    return lax.rem(me + 1, count), lax.rem(me + count - 1, count)


def halo_kernel(
    s_ref, a_ref, tab_ref, cell_ref,
    y_low, y_up, ya_up, grid_sums, axis_ext, xs, face_sums,
    x_send_up, x_send_down, x_low, x_up, z_send_up, z_send_down, z_low, z_up,
    total, work, tables, outgoing, incoming, send_sem, recv_sem, cell_send, cell_recv,
):
    rows = 136
    lane = iota((8, TILE), 1)
    sub = iota((8, TILE), 0)
    lane_z = lane & 15

    barrier = pltpu.get_barrier_semaphore()
    count_z = lax.axis_size("gz")
    me_z = lax.axis_index("gz")
    greeted = [("gx", side) for side in neighbours("gx")]
    greeted += [("gy", side) for side in neighbours("gy")]
    greeted += [("gz", lax.rem(me_z + step, count_z)) for step in range(1, count_z)]
    for name, side in greeted:
        pl.semaphore_signal(
            barrier, inc=1, device_id={name: side}, device_id_type=pl.DeviceIdType.MESH
        )
    pl.semaphore_wait(barrier, len(greeted))

    def remote(src, dst, name, upward, slot):
        up, down = neighbours(name)
        return pltpu.make_async_remote_copy(
            src_ref=src, dst_ref=dst, send_sem=send_sem.at[slot], recv_sem=recv_sem.at[slot],
            device_id={name: up if upward else down}, device_id_type=pl.DeviceIdType.MESH,
        )

    copies = [
        remote(s_ref.at[:, :, 1, :, pl.ds(120, 8), :], y_low, "gy", True, 0),
        remote(s_ref.at[:, :, 0, :, pl.ds(0, 8), :], y_up, "gy", False, 1),
        remote(a_ref.at[pl.ds(0, 8), :], ya_up, "gy", False, 2),
    ]
    for copy in copies:
        copy.start()
    for q in range(4):
        for bx in range(2):
            for bz in range(2):
                grid_sums[q, bx, bz, 8:128, :] = (
                    s_ref[q, bx, 0, bz, 8:128, :] + s_ref[q, bx, 1, bz, 4:124, :]
                )
    axis_ext[0:128, :] = a_ref[...]
    for copy in copies:
        copy.wait()
    for q in range(4):
        for bx in range(2):
            for bz in range(2):
                grid_sums[q, bx, bz, 0:8, :] = s_ref[q, bx, 0, bz, 0:8, :] + jnp.where(
                    sub < 4,
                    roll(y_low[q, bx, bz], 4, 0),
                    roll(s_ref[q, bx, 1, bz, 0:8, :], 4, 0),
                )
                grid_sums[q, bx, bz, 128:136, :] = jnp.where(
                    sub < 4,
                    roll(s_ref[q, bx, 1, bz, 120:128, :], 4, 0) + y_up[q, bx, bz],
                    0.0,
                )
    axis_ext[128:136, :] = jnp.where(sub < 4, ya_up[...], 0.0)

    lane40 = iota((40, TILE), 1)
    zeros40 = jnp.zeros((40, TILE), F32)
    pack_up = zeros40
    pack_down = zeros40
    fill = jnp.zeros((6, TILE), F32)
    for q in range(4):
        for bz in range(2):
            i = q * 2 + bz
            xs[i, 0:8, :] = jnp.zeros((8, TILE), F32)
            xs[i, 136:144, :] = jnp.zeros((8, TILE), F32)
            xs[i, 1:137, :] = roll(grid_sums[q, 1, bz], 16)
            up_rows = jnp.concatenate([xs[i, pl.ds(4, 34, stride=4), :], fill], axis=0)
            down_rows = jnp.concatenate([grid_sums[q, 0, bz, pl.ds(0, 34, stride=4), :], fill], axis=0)
            slot = (lane40 >> 4) == i
            pack_up = jnp.where(slot, roll(up_rows, 16 * i), pack_up)
            pack_down = jnp.where(slot, roll(down_rows, 16 * i), pack_down)
    x_send_up[...] = pack_up
    x_send_down[0] = pack_down
    x_send_down[1] = jnp.concatenate([axis_ext[pl.ds(0, 34, stride=4), :], fill], axis=0)
    copies = [
        remote(x_send_up, x_low, "gx", True, 3),
        remote(x_send_down, x_up, "gx", False, 4),
    ]
    for copy in copies:
        copy.start()
    for copy in copies:
        copy.wait()
    lane_r = iota((rows, TILE), 1)
    from_low = x_low[...]
    for q in range(4):
        for bz in range(2):
            i = q * 2 + bz
            ring = roll(grid_sums[q, 1, bz], 16)
            xs[i, pl.ds(0, 34, stride=4), :] = roll(from_low, -16 * i)[0:34]
            face_sums[q, bz] = grid_sums[q, 0, bz] + jnp.where(lane_r >= 16, ring, xs[i, 0:136, :])
    x32 = pack_up + x_up[0]
    ax32 = x_up[1]

    def squeeze(load, z_pos):
        first = jnp.zeros((8, TILE), F32)
        for k in range(16):
            first = jnp.where(lane_z == k, roll(load(8 * k), k - z_pos), first)
        second = roll(load(128), -z_pos)
        return first, second

    def squeeze_edge(value, from_lane):
        out = jnp.zeros((8, TILE), F32)
        for g in range(5):
            out = jnp.where((lane & 31) == g, roll(value[8 * g : 8 * g + 8], g - from_lane), out)
        return out

    for q in range(4):
        z_send_up[q], z_send_up[4 + q] = squeeze(lambda r: face_sums[q, 1, r : r + 8, :], 15)
        z_send_down[q], z_send_down[4 + q] = squeeze(lambda r: face_sums[q, 0, r : r + 8, :], 0)
    z_send_up[8] = squeeze_edge(x32, 31)
    z_send_down[8] = squeeze_edge(x32, 0)
    z_send_down[9], z_send_down[10] = squeeze(lambda r: axis_ext[r : r + 8, :], 0)
    z_send_down[11] = squeeze_edge(ax32, 0)
    copies = [
        remote(z_send_up, z_low, "gz", True, 5),
        remote(z_send_down, z_up, "gz", False, 6),
    ]
    for copy in copies:
        copy.start()
    for copy in copies:
        copy.wait()

    def spread(buf, q, k):
        return roll(buf[q], -k) if k < 16 else buf[4 + q]

    for q in range(4):
        for k in range(17):
            r = 8 * k
            one = face_sums[q, 1, r : r + 8, :]
            total[0, q, r : r + 8, :] = face_sums[q, 0, r : r + 8, :] + jnp.where(
                lane_z == 0, spread(z_low, q, k), roll(one, 1)
            )
            total[1, q, r : r + 8, :] = roll(one, -15) + spread(z_up, q, k)
    edge = []
    ax_edge = []
    for g in range(5):
        one = x32[8 * g : 8 * g + 8]
        part = lane & 31
        main = one + jnp.where(part == 0, roll(z_low[8], -g), roll(one, -15))
        last = roll(one, -15) + roll(z_up[8], 16 - g)
        edge.append(jnp.where(part == 16, last, main))
        ax_edge.append(jnp.where(lane == 16, roll(z_up[11], 16 - g), ax32[8 * g : 8 * g + 8]))
    edge = jnp.concatenate(edge, axis=0)
    ax_edge = jnp.concatenate(ax_edge, axis=0)

    edge_count = jnp.maximum(roll(edge, -96), 1.0)
    scale = [1.0 / jnp.maximum(total[f, 3], 1.0) for f in range(2)]
    axis_top = jnp.concatenate(
        [roll(z_up[9], -k) for k in range(16)] + [z_up[10]], axis=0
    )
    pick = jnp.clip(lane_r - 32, 0, 7) * 16
    for c in range(4):
        if c < 3:
            inner = total[0, c] * scale[0]
            top = total[1, c] * scale[1]
            side = roll(edge, -32 * c) / edge_count
        else:
            inner, top, side = axis_ext[...], axis_top, ax_edge
        work[0:136, :] = jnp.where(lane_r < 16, inner, roll(top, 16))
        work[136:144, :] = jnp.zeros((8, TILE), F32)
        work[pl.ds(4, 34, stride=4), :] = side[0:34]
        rim = jnp.where(lane_r <= 16, work[1:137, :], take(top, pick))
        if c < 3:
            tables[0, c] = inner
            tables[1, c] = rim
        else:
            in_range = jnp.where((lane_r <= 16) | ((lane_r >= 32) & (lane_r < 40)), rim, 0.0)
            for f, value in enumerate((inner, in_range)):
                for d, vec in enumerate(axis_vectors(value)):
                    tables[f, 3 + d] = vec
    for by in range(2):
        tab_ref[by] = tables[:, :, 4 * by : 4 * by + 128, :]

    xl = lane >> 4

    def cell_group(r, slot, row):
        sums = [jnp.zeros((8, TILE), F32) for _ in range(3)]
        number = jnp.zeros((8, TILE), F32)
        for bx in range(2):
            for bz in range(2):
                x_new, z_new = xl + bx, lane_z + bz
                outside = (x_new == 8) | (z_new == 16)
                rim_at = jnp.where(x_new == 8, z_new, 32 + x_new)
                index = jnp.where(outside, rim_at, (lane + 16 * bx + bz) & 127)
                for by in range(2):
                    got = []
                    for c in range(6):
                        main = tab_ref[by, 0, c, pl.ds(r, 8), :]
                        if bx or bz:
                            rim = tab_ref[by, 1, c, pl.ds(r, 8), :]
                            main = jnp.where(outside, take(rim, index), take(main, index))
                        got.append(main)
                    count = s_ref[3, bx, by, bz, pl.ds(r, 8), :]
                    number = number + count
                    drift = [count * got[c] for c in range(3)]
                    offset = [s_ref[c, bx, by, bz, pl.ds(r, 8), :] - drift[c] for c in range(3)]
                    turned = rotate(offset, got[3:6])
                    sums = [sums[c] + drift[c] + turned[c] for c in range(3)]
        inverse = 1.0 / jnp.maximum(number, 1.0)
        for c in range(3):
            outgoing[slot, c, pl.ds(row, 8), :] = sums[c] * inverse

    share = outgoing.shape[2]
    sent = []
    for step in list(range(1, count_z)) + [0]:
        owner = lax.rem(me_z + step, count_z)

        @pl.loop(0, share // 8)
        def _(k):
            row = pl.multiple_of(k * 8, 8)
            cell_group(pl.multiple_of(owner * share + row, 8), step, row)

        if step:
            copy = pltpu.make_async_remote_copy(
                src_ref=outgoing.at[step], dst_ref=incoming.at[step - 1],
                send_sem=cell_send.at[step - 1], recv_sem=cell_recv.at[step - 1],
                device_id={"gz": owner}, device_id_type=pl.DeviceIdType.MESH,
            )
            copy.start()
            sent.append(copy)
    cell_ref[me_z] = outgoing[0]
    for step in range(1, count_z):
        sent[step - 1].wait()
        cell_ref[lax.rem(me_z + count_z - step, count_z)] = incoming[step - 1]


def collide_group(group, shift_ref, place_ref, v_ref, tab_ref, out_ref):
    sub = iota((8, TILE), 0)
    tiles = pl.ds(pl.multiple_of(group * 8, 8), 8)
    base = group * (8 * PPC * TILE)
    for chunk in range(PPC):
        place = place_ref[pl.ds(group * (8 * PPC) + chunk, 8, stride=PPC), :]
        bit_x, bit_y, bit_z = shift_bits(place, shift_ref)
        cell = place >> 6
        x_new = (cell >> 4) + bit_x
        z_new = (cell & 15) + bit_z
        outside = (x_new == 8) | (z_new == 16)
        rim_at = jnp.where(x_new == 8, z_new, 32 + x_new)
        index = jnp.where(outside, rim_at, (cell + 16 * bit_x + bit_z) & 127)
        upper = bit_y == 1
        got = []
        for c in range(6):
            low = jnp.where(outside, take(tab_ref[0, 1, c, tiles, :], index), take(tab_ref[0, 0, c, tiles, :], index))
            high = jnp.where(outside, take(tab_ref[1, 1, c, tiles, :], index), take(tab_ref[1, 0, c, tiles, :], index))
            got.append(jnp.where(upper, high, low))
        speed = []
        for c in range(3):
            value = jnp.zeros((8, TILE), F32)
            for tile in range(8):
                at = pl.ds(pl.multiple_of(base + (tile * PPC + chunk) * TILE, TILE), TILE)
                value = jnp.where(
                    sub == tile, jnp.broadcast_to(v_ref[c : c + 1, at], (8, TILE)), value
                )
            speed.append(value)
        turned = rotate([speed[c] - got[c] for c in range(3)], got[3:6])
        for c in range(3):
            value = got[c] + turned[c]
            for tile in range(8):
                at = pl.ds(pl.multiple_of(base + (tile * PPC + chunk) * TILE, TILE), TILE)
                out_ref[c : c + 1, at] = value[tile : tile + 1]


def deposit(grid_shift, place, velocity, tiles):
    rows = 8 * PPC
    return pl.pallas_call(
        deposit_kernel,
        grid=(tiles // 8,),
        in_specs=[
            pl.BlockSpec(memory_space=pltpu.SMEM),
            pl.BlockSpec((rows, TILE), lambda i: (i, 0)),
            pl.BlockSpec((3, rows * TILE), lambda i: (0, i)),
        ],
        out_specs=pl.BlockSpec((4, 8, 8, TILE), lambda i: (0, 0, i, 0)),
        out_shape=jax.ShapeDtypeStruct((4, 8, tiles, TILE), F32),
        name="deposit",
    )(grid_shift, place, velocity)


def halo(sums, axis, tiles):
    dma = pltpu.SemaphoreType.DMA
    count_z = lax.axis_size("gz")
    share = tiles // count_z
    return pl.pallas_call(
        halo_kernel,
        in_specs=[pl.BlockSpec(memory_space=VMEM)] * 2,
        out_specs=[pl.BlockSpec(memory_space=VMEM)] * 2,
        out_shape=[
            jax.ShapeDtypeStruct((2, 2, 6, tiles, TILE), F32),
            jax.ShapeDtypeStruct((count_z, 3, share, TILE), F32),
        ],
        scratch_shapes=[
            VMEM((4, 2, 2, 8, TILE), F32),
            VMEM((4, 2, 2, 8, TILE), F32),
            VMEM((8, TILE), F32),
            VMEM((4, 2, 2, 136, TILE), F32),
            VMEM((136, TILE), F32),
            VMEM((8, 144, TILE), F32),
            VMEM((4, 2, 136, TILE), F32),
            VMEM((40, TILE), F32),
            VMEM((2, 40, TILE), F32),
            VMEM((40, TILE), F32),
            VMEM((2, 40, TILE), F32),
            VMEM((9, 8, TILE), F32),
            VMEM((12, 8, TILE), F32),
            VMEM((9, 8, TILE), F32),
            VMEM((12, 8, TILE), F32),
            VMEM((2, 4, 136, TILE), F32),
            VMEM((144, TILE), F32),
            VMEM((2, 6, 136, TILE), F32),
            VMEM((count_z, 3, share, TILE), F32),
            VMEM((count_z - 1, 3, share, TILE), F32),
            dma((7,)),
            dma((7,)),
            dma((count_z - 1,)),
            dma((count_z - 1,)),
        ],
        compiler_params=pltpu.CompilerParams(collective_id=0, has_side_effects=True),
        name="halo",
    )(sums, axis)


def exchange_kernel(
    shift_ref, place_ref, v_ref, tab_ref, x_ref, out_ref, new_ref, send_sem, recv_sem
):
    count_y, count_z = lax.axis_size("gy"), lax.axis_size("gz")
    me_y, me_z = lax.axis_index("gy"), lax.axis_index("gz")
    me = me_y * count_z + me_z
    peers = [
        (lax.rem(me_y + dy, count_y), lax.rem(me_z + dz, count_z))
        for dy in range(count_y)
        for dz in range(count_z)
        if dy or dz
    ]
    barrier = pltpu.get_barrier_semaphore()
    for y, z in peers:
        pl.semaphore_signal(
            barrier, inc=1, device_id={"gy": y, "gz": z}, device_id_type=pl.DeviceIdType.MESH
        )
    pl.semaphore_wait(barrier, len(peers))
    copies = [
        pltpu.make_async_remote_copy(
            src_ref=x_ref.at[y * count_z + z], dst_ref=out_ref.at[me],
            send_sem=send_sem.at[slot], recv_sem=recv_sem.at[slot],
            device_id={"gy": y, "gz": z}, device_id_type=pl.DeviceIdType.MESH,
        )
        for slot, (y, z) in enumerate(peers)
    ]
    for copy in copies:
        copy.start()
    out_ref[me] = x_ref[me]

    @pl.loop(0, place_ref.shape[0] // (16 * PPC))
    def _(group):
        collide_group(group, shift_ref, place_ref, v_ref, tab_ref, new_ref)

    for copy in copies:
        copy.wait()


def exchange(grid_shift, place, velocity, tables, blocks):
    peers = blocks.shape[0] - 1
    dma = pltpu.SemaphoreType.DMA
    return pl.pallas_call(
        exchange_kernel,
        in_specs=particle_specs() + [pl.BlockSpec(memory_space=VMEM)],
        out_specs=[pl.BlockSpec(memory_space=VMEM)] * 2,
        out_shape=[
            jax.ShapeDtypeStruct(blocks.shape, F32),
            jax.ShapeDtypeStruct((3, velocity.shape[1] // 2), F32),
        ],
        scratch_shapes=[dma((peers,)), dma((peers,))],
        compiler_params=pltpu.CompilerParams(collective_id=2, has_side_effects=True),
        name="exchange",
    )(grid_shift, place, velocity, tables, blocks)


def final_kernel(
    lengths, shells, shift_ref, place_ref, v_ref, tab_ref, done_ref, block_ref, phase_ref, n_ref,
    new_ref, m_ref, out_ref,
    arrived, bins, mine, others, block_send, block_recv, send_sem, recv_sem,
):
    groups = place_ref.shape[0] // (8 * PPC)
    cuts = [groups // 2, groups * 5 // 8, groups * 7 // 8, groups]

    def collide_some(part):
        @pl.loop(cuts[part], cuts[part + 1])
        def _(group):
            collide_group(group, shift_ref, place_ref, v_ref, tab_ref, new_ref)

    names = ("gx", "gy", "gz")
    sizes = [lax.axis_size(name) for name in names]
    at = [lax.axis_index(name) for name in names]
    peers = []
    for dx in range(sizes[0]):
        for dy in range(sizes[1]):
            for dz in range(sizes[2]):
                if dx or dy or dz:
                    peers.append(
                        tuple(lax.rem(at[d] + step, sizes[d]) for d, step in enumerate((dx, dy, dz)))
                    )
    barrier = pltpu.get_barrier_semaphore()
    for peer in peers:
        pl.semaphore_signal(
            barrier, inc=1, device_id=peer, device_id_type=pl.DeviceIdType.MESH
        )
    collide_some(0)
    new_ref[:, 0 : done_ref.shape[1]] = done_ref[...]
    pl.semaphore_wait(barrier, len(peers))
    blocks = []
    for step in range(1, sizes[0]):
        target = lax.rem(at[0] + step, sizes[0])
        copy = pltpu.make_async_remote_copy(
            src_ref=block_ref.at[target], dst_ref=arrived.at[step - 1],
            send_sem=block_send.at[step - 1], recv_sem=block_recv.at[step - 1],
            device_id={"gx": target}, device_id_type=pl.DeviceIdType.MESH,
        )
        copy.start()
        blocks.append(copy)
    collide_some(1)
    for copy in blocks:
        copy.wait()
    length_x, length_y, length_z = lengths
    half = block_ref.shape[1]
    modes = jnp.zeros((half, 4 * length_x), F32)
    for step in range(sizes[0]):
        source = lax.rem(at[0] + sizes[0] - step, sizes[0])
        value = arrived[step - 1] if step else block_ref[source]
        high = value.astype(jnp.bfloat16)
        low = (value - high.astype(F32)).astype(jnp.bfloat16)
        for left, right in ((high, 0), (low, 0), (high, 1)):
            modes = modes + jnp.dot(left, phase_ref[right, source], preferred_element_type=F32)
    for h in range(2):
        for part in range(2):
            at_lane = (2 * h + part) * length_x
            m_ref[part, h * half : (h + 1) * half, :] = modes[:, at_lane : at_lane + length_x]
    rows = 2 * half // 3
    depth_y = length_y // sizes[0]
    depth_z = length_z // (sizes[1] * sizes[2])
    energy = jnp.zeros((rows, length_x), F32)
    for part in range(2):
        for c in range(3):
            value = m_ref[part, c * rows : (c + 1) * rows, :]
            energy = energy + value * value
    row = iota((rows, length_x), 0)
    kz = (at[1] * sizes[2] + at[2]) * depth_z + lax.div(row, depth_y)
    ky = at[0] * depth_y + lax.rem(row, depth_y)
    kx = iota((rows, length_x), 1)
    square = jnp.zeros((rows, length_x), jnp.int32)
    for wave, length in ((kx, length_x), (ky, length_y), (kz, length_z)):
        signed = jnp.where(wave >= length // 2, wave - length, wave)
        square = square + signed * signed
    shell = jnp.floor(jnp.sqrt(square.astype(F32))).astype(jnp.int32)
    shell = jnp.where((shell + 1) * (shell + 1) <= square, shell + 1, shell)
    shell = jnp.where(shell * shell > square, shell - 1, shell)
    for s in range(shells):
        member = shell == s
        bins[s : s + 1, :] = jnp.sum(jnp.where(member, energy, 0.0), axis=0, keepdims=True)
    width = bins.shape[1]
    diagonal = iota((shells, width), 0) == iota((shells, width), 1)
    column = jnp.sum(bins[...], axis=1, keepdims=True)
    line = jnp.sum(jnp.where(diagonal, column, 0.0), axis=0, keepdims=True)
    packed = jnp.broadcast_to(line, (8, width))
    mine[...] = packed
    copies = [
        pltpu.make_async_remote_copy(
            src_ref=mine, dst_ref=others.at[slot], send_sem=send_sem.at[slot],
            recv_sem=recv_sem.at[slot], device_id=peer, device_id_type=pl.DeviceIdType.MESH,
        )
        for slot, peer in enumerate(peers)
    ]
    for copy in copies:
        copy.start()
    collide_some(2)
    for copy in copies:
        copy.wait()
    total = packed + jnp.sum(others[...], axis=0)
    out_ref[...] = total / n_ref[...]


def particle_specs():
    return [
        pl.BlockSpec(memory_space=pltpu.SMEM),
    ] + [pl.BlockSpec(memory_space=VMEM)] * 3


def finish(grid_shift, place, velocity, tables, done, blocks, phases, lengths):
    shells = min(lengths) // 2
    width = lengths[0]
    count_x = lax.axis_size("gx")
    count = count_x * lax.axis_size("gy") * lax.axis_size("gz")
    dma = pltpu.SemaphoreType.DMA
    half = blocks.shape[1]
    waves = [np.minimum(np.arange(n), n - np.arange(n)) ** 2 for n in lengths]
    square = waves[2][:, None, None] + waves[1][None, :, None] + waves[0][None, None, :]
    shell = np.floor(np.sqrt(square.astype(np.float64))).astype(np.int64).ravel()
    number = np.ones((8, width), np.float32)
    number[:, :shells] = np.bincount(shell, minlength=shells)[:shells]
    whole = pl.BlockSpec(memory_space=VMEM)
    new_velocity, modes, out = pl.pallas_call(
        functools.partial(final_kernel, lengths, shells),
        in_specs=particle_specs() + [whole] * 4,
        out_specs=[whole] * 3,
        out_shape=[
            jax.ShapeDtypeStruct(velocity.shape, F32),
            jax.ShapeDtypeStruct((2, 2 * half, width), F32),
            jax.ShapeDtypeStruct((8, width), F32),
        ],
        scratch_shapes=[
            VMEM((count_x - 1, half, blocks.shape[2]), F32),
            VMEM((shells, width), F32),
            VMEM((8, width), F32),
            VMEM((count - 1, 8, width), F32),
            dma((count_x - 1,)),
            dma((count_x - 1,)),
            dma((count - 1,)),
            dma((count - 1,)),
        ],
        compiler_params=pltpu.CompilerParams(collective_id=1, has_side_effects=True),
        name="finish",
    )(grid_shift, place, velocity, tables, done, blocks, phases, jnp.asarray(number))
    return new_velocity, modes, out[0, :shells]


def phase_tables(positions, length):
    steps = positions[..., None] * np.arange(length) % length
    angle = steps * (2.0 * math.pi / length)
    return np.cos(angle).astype(np.float32), np.sin(angle).astype(np.float32)


def per_device(velocity, particle_place, grid_shift, rotation_axis):
    size_y, size_x, size_z = rotation_axis.shape
    cell_count = size_y * size_x * size_z
    tile_count = cell_count // TILE
    place = particle_place.reshape(tile_count * PPC, TILE)
    sums = deposit(grid_shift, place, velocity, tile_count)
    axis = rotation_axis.reshape(tile_count, TILE).astype(F32)
    tables, cell_sums = halo(sums.reshape(4, 2, 2, 2, tile_count, TILE), axis, tile_count)
    count_x = lax.axis_size("gx")
    count_y = lax.axis_size("gy")
    count_z = lax.axis_size("gz")
    rows_y = size_y // count_z
    length_x = size_x * count_x
    length_y = size_y * count_y
    length_z = size_z * count_z
    arrived = cell_sums.reshape(count_z, 3, rows_y, size_x, size_z)
    cos_z, sin_z = phase_tables(np.arange(length_z).reshape(count_z, size_z), length_z)
    both_z = np.stack([cos_z, -sin_z], axis=-1)
    stacked_z = jnp.einsum("gcyxz,gzkp->kpcyx", arrived, both_z, precision=HIGH)
    depth_z = length_z // (count_y * count_z)
    blocks = stacked_z.reshape(count_y * count_z, -1, TILE)
    pencil, done = exchange(grid_shift, place, velocity, tables, blocks)
    pencil = pencil.reshape(count_y, count_z, depth_z, 2, 3, rows_y, size_x)
    cos_y, sin_y = phase_tables(np.arange(length_y).reshape(count_y, count_z, rows_y), length_y)
    both_y = np.stack([np.stack([cos_y, -sin_y]), np.stack([sin_y, cos_y])])
    depth_y = length_y // count_x
    half = 3 * depth_z * depth_y // 2
    stacked_y = jnp.einsum("abzpcyx,pqabyk->czkqx", pencil, both_y, precision=HIGH)
    blocks = stacked_y.reshape(3, depth_z, count_x, depth_y, 2 * size_x)
    blocks = blocks.transpose(2, 0, 1, 3, 4).reshape(count_x, 2, half, 2 * size_x)
    blocks = blocks.transpose(0, 2, 1, 3).reshape(count_x, half, 4 * size_x)
    cos_x, sin_x = phase_tables(np.arange(length_x).reshape(count_x, size_x), length_x)
    norm_scale = 1.0 / math.sqrt(length_x * length_y * length_z)
    both_x = np.stack([np.stack([cos_x, -sin_x]), np.stack([sin_x, cos_x])]) * norm_scale
    both_x = both_x.transpose(2, 0, 3, 1, 4).reshape(count_x, 2 * size_x, 2 * length_x)
    phases = np.zeros((count_x, 4 * size_x, 4 * length_x), np.float32)
    phases[:, : 2 * size_x, : 2 * length_x] = both_x
    phases[:, 2 * size_x :, 2 * length_x :] = both_x
    high = phases.astype(jnp.bfloat16)
    low = (phases - high.astype(np.float32)).astype(jnp.bfloat16)
    new_velocity, modes, spectrum = finish(
        grid_shift, place, velocity, tables, done, blocks, jnp.asarray(np.stack([high, low])),
        (length_x, length_y, length_z),
    )
    return (new_velocity, modes.reshape(2, 3, depth_z, depth_y, length_x), spectrum)


def solution(mesh):
    placed = (P(None, ("gx", "gy", "gz")), P(("gx", "gy", "gz")), P(), P("gy", "gx", "gz"))
    return jax.shard_map(
        per_device,
        mesh=mesh,
        in_specs=placed,
        out_specs=(P(None, ("gx", "gy", "gz")), P(None, None, ("gy", "gz"), "gx", None), P()),
        check_vma=False,
    )
```
